256 devices in a mesh: tm: 8 (over x, y_lo), space: 32 (over z, y_hi, core).
Axes of the slice: x: 4, y: 4 (y_hi: 2, y_lo: 2; y = y_hi * 2 + y_lo), z: 8, core: 2. Of those that a mesh axis runs over, the one named last changes fastest.
Arguments:
- iterate: float32 [64, 5, 65536], P('tm', None, 'space'), may hold values from -6 to 6
- right_side: float32 [64, 5, 65536], P('tm', None, 'space'), may hold values from -6 to 6
- jacobian: float32 [6, 5, 5, 65536], P(None, None, None, 'space'), may hold values from -0.24 to 0.24
- self_block: float32 [5, 5, 65536], P(None, None, 'space'), may hold values from -0.48 to 0.48
- cell_diag: float32 [5, 65536], P(None, 'space'), may hold values from 2.5 to 5
- neighbours: int32 [512, 6], P('space'), may hold values from 0 to 31, as said below
- face_list: int32 [256], P('space'), may hold values from 0 to 15, as said below
Outputs:
- updated: float32 [64, 5, 65536], P('tm', None, 'space')
- residual: float32 [64, 5, 65536], P('tm', None, 'space')
The draws below stay inside these ranges and needn't reach their ends.
Inputs may be any that keep to these rules, and one draw needn't show every extreme that they name: `neighbours`: row b of slab s names 6 blocks in slab s's extended numbering: 0 to 15 its own blocks, 16 + h the h-th face block of slab s-1, 24 + h the h-th face block of slab s+1. Entry 0 always names a face block of the lower slab, entry 1 one of the upper slab, entries 2 to 5 own blocks. `face_list`: each slab's 8 entries are distinct local blocks of that slab; the last entry is always the slab's last block.
All inputs are finite; a program needn't handle non-finite values.
Results may differ from the reference program's by a relative error of at most 0.0001.
Values sent between devices are 32-bit elements; how exact they have to be, the bound alone decides.
A program may use at most 64 MiB of HBM per device.

```python
import math
import jax
import jax.numpy as jnp

NV = 5
BLK = 128
K = 6
NT = 64
NU1 = 2
NU2 = 2
NUC = 4
BD = 16
H = 8
NTC = 16
NB = 512
NC = 65536
FACES = 256
N_SPACE = 32


def draw_neighbours(key, part):
    shard_count = NB // BD
    keys = jax.random.split(key, 4)
    lower_shift = jax.random.randint(keys[0], (shard_count, 1), 0, H)
    upper_shift = jax.random.randint(keys[1], (shard_count, 1), 0, H)
    local = jnp.arange(BD, dtype=jnp.int32)[None, :]
    first = BD + (local + lower_shift) % H
    second = BD + H + (BD - 1 - local + upper_shift) % H
    third = jax.vmap(lambda sub_key: jax.random.permutation(sub_key, BD))(jax.random.split(keys[2], shard_count))
    others = jax.random.randint(keys[3], (shard_count, BD, K - 3), 0, BD)
    table = jnp.concatenate([first[:, :, None].astype(jnp.int32), second[:, :, None].astype(jnp.int32), third[:, :, None].astype(jnp.int32), others.astype(jnp.int32)], axis=2)
    return table.reshape(NB, K).astype(jnp.int32)


def draw_face_list(key, part):
    shard_count = FACES // H

    def one_slab(sub_key):
        chosen = jax.random.permutation(sub_key, BD - 1)[:H - 1].astype(jnp.int32)
        return jnp.concatenate([chosen, jnp.full((1,), BD - 1, jnp.int32)])
    return jax.vmap(one_slab)(jax.random.split(key, shard_count)).reshape(FACES).astype(jnp.int32)


def block_scale(rng, dims, shards, smallest, largest):
    gain = 1.0
    for dim, shards_of in shards:
        draws = jax.random.uniform(jax.random.fold_in(jax.random.fold_in(rng, 6), dim), (shards_of,), jnp.float32, smallest / len(shards), largest / len(shards))
        gain = gain * jnp.repeat(jnp.exp(draws), dims[dim] // shards_of).reshape((-1,) + (1,) * (len(dims) - 1 - dim))
    return gain


def noise(key, shape, spread, limit, cuts=(), kind=jnp.bfloat16):
    level = block_scale(key, shape, cuts, -0.22, 0.18) if cuts else 1.0
    array = jax.random.normal(key, shape, jnp.float32) * spread * level
    return jnp.minimum(jnp.maximum(array, -limit), limit).astype(kind)


def setup_inputs(seed: int = 0) -> dict:
    arg_keys = jax.random.split(jax.random.key(seed), 8)
    return {
        "iterate": noise(arg_keys[0], (NT, NV, NC), 1.0, 6.0, ((0, 8), (2, 32)), jnp.float32),
        "right_side": noise(arg_keys[1], (NT, NV, NC), 1.0, 6.0, ((0, 8), (2, 32)), jnp.float32),
        "jacobian": noise(arg_keys[2], (K, NV, NV, NC), 0.04, 0.24, ((3, 32),), jnp.float32),
        "self_block": noise(arg_keys[3], (NV, NV, NC), 0.08, 0.48, ((2, 32),), jnp.float32),
        "cell_diag": jnp.clip(jnp.exp(math.log(5.0) - 0.6931472 * jax.random.uniform(arg_keys[4], (NV, NC), jnp.float32) ** block_scale(arg_keys[4], (NV, NC), ((1, 32),), -0.2, 0.2)), 2.5, 5.0),
        "neighbours": draw_neighbours(jax.random.fold_in(arg_keys[7], 71), 0),
        "face_list": draw_face_list(jax.random.fold_in(arg_keys[7], 71), 0),
    }


time_weight = 0.5
damping = 0.7


def pick_blocks(blocks, block_index):
    return jax.vmap(lambda part_blocks, chosen: jnp.take(part_blocks, chosen, axis=2), in_axes=(2, 0), out_axes=2)(blocks, block_index)


def space_term(field, jacobian, self_block, cell_diag, neighbours, face_list):
    step_count = field.shape[0]
    blocks = field.reshape(step_count, NV, N_SPACE, BD, BLK)
    outgoing = pick_blocks(blocks, face_list.reshape(N_SPACE, H))
    empty = jnp.zeros_like(outgoing[:, :, :1])
    lower_rim = jnp.concatenate([empty, outgoing[:, :, :-1]], axis=2)
    upper_rim = jnp.concatenate([outgoing[:, :, 1:], empty], axis=2)
    extended = jnp.concatenate([blocks, lower_rim, upper_rim], axis=3)
    slot_table = neighbours.reshape(N_SPACE, BD, K)
    off_diag = self_block * (1.0 - jnp.eye(NV, dtype=jnp.float32))[:, :, None]
    summed = jnp.sum(off_diag[None] * field[:, None], axis=2) + cell_diag[None] * field
    for neighbour_slot in range(K):
        picked = pick_blocks(extended, slot_table[:, :, neighbour_slot]).reshape(step_count, NV, N_SPACE * BD * BLK)
        summed = summed + jnp.sum(jacobian[neighbour_slot][None] * picked[:, None], axis=2)
    return summed


def operator(field, weight, jacobian, self_block, cell_diag, neighbours, face_list):
    back_one = jnp.roll(field, 1, axis=0)
    back_two = jnp.roll(field, 2, axis=0)
    timed = weight * (3.0 * field - 4.0 * back_one + back_two)
    return timed + space_term(field, jacobian, self_block, cell_diag, neighbours, face_list)


def reference(iterate, right_side, jacobian, self_block, cell_diag, neighbours, face_list):
    extra = (jacobian, self_block, cell_diag, neighbours, face_list)
    inverse_fine = 1.0 / (3.0 * time_weight + cell_diag)
    coarse_weight = time_weight / 4.0
    inverse_coarse = 1.0 / (3.0 * coarse_weight + cell_diag)
    state = iterate
    for sweep_no in range(NU1):
        state = state + damping * inverse_fine * (right_side - operator(state, time_weight, *extra))
    defect = right_side - operator(state, time_weight, *extra)
    coarse_defect = defect.reshape(NTC, 4, NV, NC).mean(axis=1)
    correction = damping * inverse_coarse * coarse_defect
    for sweep_no in range(NUC - 1):
        correction = correction + damping * inverse_coarse * (coarse_defect - operator(correction, coarse_weight, *extra))
    state = state + jnp.repeat(correction, 4, axis=0)
    for sweep_no in range(NU2):
        state = state + damping * inverse_fine * (right_side - operator(state, time_weight, *extra))
    residual = right_side - operator(state, time_weight, *extra)
    return state, residual
```

```python
import functools

import jax
import jax.numpy as jnp
from jax import lax
from jax.experimental import pallas as pl
from jax.experimental.pallas import tpu as pltpu
from jax.sharding import PartitionSpec as P

NV = 5
BLK = 128
K = 6
BD = 16
H = 8
T = 8

WEIGHT = 0.5
COARSE = WEIGHT / 4.0
DAMP = 0.7
MESH = pl.DeviceIdType.MESH

FINE = ("f1", "f2", "f3", "f5", "f6")
SMALL = ("c0", "c1", "c2", "c3", "c4")
RING = ("f1", "f2", "f3", "f5", "f6", "c1", "c2", "c3", "c4")


def roll(x, n):
    return pltpu.roll(x, n % T, axis=0)


def kernel(n_tm, n_space, names, *refs):
    r = dict(zip(names, refs))
    tm = lax.axis_index("tm")
    slab = lax.axis_index("space")
    core = lax.rem(slab, 2)
    near_dev = (tm, slab + 1 - 2 * core)
    far_slab = slab - 1 + 2 * core
    has_far = jnp.logical_and(far_slab >= 0, far_slab < n_space)
    far_dev = (tm, far_slab)
    next_dev = (lax.rem(tm + 1, n_tm), slab)
    prev_dev = (lax.rem(tm + n_tm - 1, n_tm), slab)
    near_slot = 1 - core
    far_slot = core
    nb, fl = r["nb"], r["fl"]
    jac, sb, dg = r["jac"], r["sb"], r["dg"]
    v, pre, rhs = r["v"], r["pre"], r["rhs"]
    cf, cc = r["cf"], r["cc"]
    corr, cpre, cd = r["corr"], r["cpre"], r["cd"]

    sub = lax.broadcasted_iota(jnp.int32, (T, BLK), 0)
    sub4 = lax.rem(sub, 4)

    barrier = pltpu.get_barrier_semaphore()
    for dev in (near_dev, next_dev, prev_dev):
        pl.semaphore_signal(barrier, inc=1, device_id=dev, device_id_type=MESH)

    @pl.when(has_far)
    def _():
        pl.semaphore_signal(barrier, inc=1, device_id=far_dev, device_id_type=MESH)

    loads = {}
    for i, (src, dst) in enumerate(
        (("v_in", "v"), ("jac_in", "jac"), ("rhs_in", "rhs"), ("sb_in", "sb"), ("dg_in", "dg"))
    ):
        loads[dst] = pltpu.make_async_copy(r[src], r[dst], r["load_sem"].at[i])
        loads[dst].start()

    sem_index = {}
    for name in FINE + SMALL:
        for side in ("near", "far"):
            sem_index[name, side] = len(sem_index)
    for name in RING:
        sem_index[name, "ring"] = len(sem_index)

    def copy_of(name, side):
        i = sem_index[name, side]
        dev = {"near": near_dev, "far": far_dev, "ring": next_dev}[side]
        src = r["ring_out_" + name] if side == "ring" else r["face_out_" + name]
        return pltpu.make_async_remote_copy(
            src_ref=src,
            dst_ref=r[side + "_in_" + name],
            send_sem=r["send_sem"].at[i],
            recv_sem=r["recv_sem"].at[i],
            device_id=dev,
            device_id_type=MESH,
        )

    def send_faces(name):
        @pl.when(has_far)
        def _():
            copy_of(name, "far").start()

        copy_of(name, "near").start()

    def wait(name, side):
        if side == "far":

            @pl.when(has_far)
            def _():
                copy_of(name, side).wait_recv()

        else:
            copy_of(name, side).wait_recv()

    def row(ref, idx, k):
        return ref[idx + (pl.ds(k, T, stride=0), slice(None))]

    def own_block(b, x, g, field, three_w, timed):
        acc = []
        for a in range(NV):
            t = g[a] - (row(dg, (b,), a) + three_w) * x[a]
            t = t + timed(x[a])
            for j in range(NV):
                if j != a:
                    t = t - row(sb, (a, b), j) * x[j]
            acc.append(t)
        for k in range(2, K):
            at = nb[k, b]
            p = [field[j, at] for j in range(NV)]
            for a in range(NV):
                for j in range(NV):
                    acc[a] = acc[a] - row(jac, (a, j, b), k) * p[j]
        return acc

    def timed_fine(x):
        zero = jnp.zeros_like(x)
        one = jnp.where(sub >= 1, roll(x, 1), zero)
        two = jnp.where(sub >= 2, roll(x, 2), zero)
        return (4.0 * WEIGHT) * one - WEIGHT * two

    def timed_coarse(x):
        return (4.0 * COARSE) * jnp.where(sub >= 4, roll(x, 4), jnp.zeros_like(x))

    def blocks(body):
        def step(b, carry):
            body(b)
            return carry

        lax.fori_loop(0, BD, step, 0)

    def own(field, g, out, three_w, timed):
        def body(b):
            x = [field[j, b] for j in range(NV)]
            acc = own_block(b, x, [g[a, b] for a in range(NV)], field, three_w, timed)
            for a in range(NV):
                out[a, b] = acc[a]

        blocks(body)

    def rim(acc, b, field, slot):
        at = jnp.bitwise_and(nb[slot, b], H - 1)
        p = [field[j, at] for j in range(NV)]
        for a in range(NV):
            for j in range(NV):
                acc[a] = acc[a] - row(jac, (a, j, b), slot) * p[j]
        return acc

    def fold_rim(out, field, slot):
        def body(b):
            acc = rim([out[a, b] for a in range(NV)], b, field, slot)
            for a in range(NV):
                out[a, b] = acc[a]

        blocks(body)

    def pack_ring(name, rows_of, place):
        out = r["ring_out_" + name]

        def body(g, carry):
            for a in range(NV):
                tile = None
                for i in range(4):
                    piece = place(rows_of(a, 4 * g + i), i)
                    tile = piece if tile is None else jnp.where(group_of(i), piece, tile)
                out[a, g] = tile
            return carry

        group_of = (lambda i: sub // 2 == i) if place is place_fine else (lambda i: sub4 == i)
        lax.fori_loop(0, BD // 4, body, 0)
        copy_of(name, "ring").start()

    def place_fine(x, i):
        q = WEIGHT * (roll(x, 2) - jnp.where(sub == 0, 4.0 * roll(x, 1), jnp.zeros_like(x)))
        return roll(q, 2 * i) if i else q

    def place_coarse(x, i):
        other = roll(x, 4)
        return COARSE * jnp.where(sub >= 4, x, x - 4.0 * other)

    def fold_ring_fine(name, out):
        src = r["ring_in_" + name]

        def body(g, carry):
            for a in range(NV):
                tile = src[a, g]
                for i in range(4):
                    q = roll(tile, T - 2 * i) if i else tile
                    out[a, 4 * g + i] = out[a, 4 * g + i] - jnp.where(sub < 2, q, jnp.zeros_like(q))
            return carry

        lax.fori_loop(0, BD // 4, body, 0)

    def spread(tile, turns, i):
        x = None
        for u in range(4):
            y = turns[u - i]
            x = y if x is None else jnp.where(sub4 == u, y, x)
        return x

    def turns_of(tile):
        return {d: (roll(tile, d) if d else tile) for d in range(-3, 4)}

    def fold_ring_coarse(name, out):
        src = r["ring_in_" + name]

        def body(g, carry):
            for a in range(NV):
                tile = src[a, g]
                turns = turns_of(tile)
                for i in range(4):
                    out[a, 4 * g + i] = out[a, 4 * g + i] - spread(tile, turns, i)
            return carry

        lax.fori_loop(0, BD // 4, body, 0)

    def unpack(name, side):
        src, out = r[side + "_in_" + name], r["rim_" + side]

        def body(a, carry):
            for g in range(H // 4):
                tile = src[a, g]
                turns = turns_of(tile)
                for i in range(4):
                    out[a, 4 * g + i] = spread(tile, turns, i)
            return carry

        lax.fori_loop(0, NV, body, 0)
        return out

    def mean4(x):
        x = x + jnp.where(lax.rem(sub, 2) == 0, roll(x, -1), roll(x, 1))
        x = x + jnp.where(sub4 < 2, roll(x, -2), roll(x, 2))
        return 0.25 * x

    def pack_faces(name, value_of):
        out = r["face_out_" + name]

        def body(g, carry):
            got = [value_of(4 * g + i) for i in range(4)]
            for a in range(NV):
                tile = got[0][a]
                for i in range(1, 4):
                    tile = jnp.where(sub4 == i, got[i][a], tile)
                out[a, g] = tile
            return carry

        lax.fori_loop(0, H // 4, body, 0)
        send_faces(name)

    def full_faces(name, value_of):
        out = r["face_out_" + name]

        def body(h, carry):
            got = value_of(h)
            for a in range(NV):
                out[a, h] = got[a]
            return carry

        lax.fori_loop(0, H, body, 0)
        send_faces(name)

    def swept(b, field, p, scale, far):
        acc = rim([p[a, b] for a in range(NV)], b, far, far_slot)
        return [field[a, b] + scale[a, b] * acc[a] for a in range(NV)]

    def store(ref, b, values):
        for a in range(NV):
            ref[a, b] = values[a]

    @pl.when(jnp.logical_not(has_far))
    def _():
        for name in FINE + SMALL:
            ref = r["far_in_" + name]

            def clear(a, carry, ref=ref):
                for i in range(ref.shape[1]):
                    ref[a, i] = jnp.zeros((T, BLK), jnp.float32)
                return carry

            lax.fori_loop(0, NV, clear, 0)

    loads["v"].wait()
    n_near = jnp.where(has_far, 4, 3)
    pl.semaphore_wait(barrier, n_near)
    full_faces("f1", lambda h: [v[a, fl[h]] for a in range(NV)])
    pack_ring("f1", lambda a, b: v[a, b], place_fine)

    for name in ("jac", "rhs", "sb", "dg"):
        loads[name].wait()

    def scales(b):
        for a in range(NV):
            d = row(dg, (b,), a)
            cf[a, b] = DAMP / (3.0 * WEIGHT + d)
            cc[a, b] = DAMP / (3.0 * COARSE + d)

    blocks(scales)

    def settle(name, out):
        wait(name, "near")
        fold_rim(out, r["near_in_" + name], near_slot)
        wait(name, "ring")
        fold_ring_fine(name, out)
        wait(name, "far")

    own(v, rhs, pre, 3.0 * WEIGHT, timed_fine)
    settle("f1", pre)
    far = r["far_in_f1"]
    full_faces("f2", lambda h, far=far: swept(fl[h], v, pre, cf, far))
    blocks(lambda b, far=far: store(v, b, swept(b, v, pre, cf, far)))
    pack_ring("f2", lambda a, b: v[a, b], place_fine)
    own(v, rhs, pre, 3.0 * WEIGHT, timed_fine)
    settle("f2", pre)
    far = r["far_in_f2"]
    pack_faces("c0", lambda h, far=far: [mean4(x) for x in swept(fl[h], v, pre, cf, far)])
    blocks(lambda b, far=far: store(v, b, swept(b, v, pre, cf, far)))
    pack_ring("f3", lambda a, b: v[a, b], place_fine)
    full_faces("f3", lambda h: [v[a, fl[h]] for a in range(NV)])

    own(v, rhs, pre, 3.0 * WEIGHT, timed_fine)
    wait("f3", "ring")
    fold_ring_fine("f3", pre)
    blocks(lambda b: store(cpre, b, [mean4(pre[a, b]) for a in range(NV)]))
    wait("c0", "near")
    fold_rim(cpre, unpack("c0", "near"), near_slot)
    wait("c0", "far")
    far = unpack("c0", "far")

    def first(b):
        acc = rim([cpre[a, b] for a in range(NV)], b, far, far_slot)
        return acc, [cc[a, b] * acc[a] for a in range(NV)]

    def first_store(b):
        acc, values = first(b)
        store(cd, b, acc)
        store(corr, b, values)

    pack_faces("c1", lambda h: first(fl[h])[1])
    blocks(first_store)
    pack_ring("c1", lambda a, b: corr[a, b], place_coarse)

    for name, later in (("c1", "c2"), ("c2", "c3"), ("c3", "c4")):
        own(corr, cd, cpre, 3.0 * COARSE, timed_coarse)
        wait(name, "near")
        fold_rim(cpre, unpack(name, "near"), near_slot)
        wait(name, "ring")
        fold_ring_coarse(name, cpre)
        if name == "c2":
            wait("f3", "near")
            fold_rim(pre, r["near_in_f3"], near_slot)
            wait("f3", "far")
            fold_rim(pre, r["far_in_f3"], far_slot)
        wait(name, "far")
        far = unpack(name, "far")
        pack_faces(later, lambda h, far=far: swept(fl[h], corr, cpre, cc, far))
        blocks(lambda b, far=far: store(corr, b, swept(b, corr, cpre, cc, far)))
        pack_ring(later, lambda a, b: corr[a, b], place_fine if later == "c4" else place_coarse)

    def correct(b):
        for a in range(NV):
            v[a, b] = v[a, b] + corr[a, b]

    own(corr, pre, pre, 3.0 * WEIGHT, timed_fine)
    blocks(correct)
    wait("c4", "near")
    fold_rim(pre, unpack("c4", "near"), near_slot)
    wait("c4", "ring")
    fold_ring_fine("c4", pre)
    wait("c4", "far")
    far = unpack("c4", "far")
    full_faces("f5", lambda h, far=far: swept(fl[h], v, pre, cf, far))
    blocks(lambda b, far=far: store(v, b, swept(b, v, pre, cf, far)))
    pack_ring("f5", lambda a, b: v[a, b], place_fine)
    own(v, rhs, pre, 3.0 * WEIGHT, timed_fine)
    settle("f5", pre)
    far = r["far_in_f5"]
    full_faces("f6", lambda h, far=far: swept(fl[h], v, pre, cf, far))
    blocks(lambda b, far=far: store(v, b, swept(b, v, pre, cf, far)))
    pack_ring("f6", lambda a, b: v[a, b], place_fine)
    save_v = pltpu.make_async_copy(v, r["v_out"], r["load_sem"].at[5])
    save_v.start()
    own(v, rhs, pre, 3.0 * WEIGHT, timed_fine)
    settle("f6", pre)
    fold_rim(pre, r["far_in_f6"], far_slot)
    save_r = pltpu.make_async_copy(pre, r["r_out"], r["load_sem"].at[6])
    save_r.start()
    for name, side in sem_index:
        if side == "far":

            @pl.when(has_far)
            def _(name=name, side=side):
                copy_of(name, side).wait_send()

        else:
            copy_of(name, side).wait_send()
    save_v.wait()
    save_r.wait()


def body(n_tm, n_space, iterate, right_side, jacobian, self_block, cell_diag, neighbours, face_list):
    def tiles(x):
        return x.reshape(T, NV, BD, BLK).transpose(1, 2, 0, 3)

    def untile(x):
        return x.transpose(2, 0, 1, 3).reshape(T, NV, BD * BLK)

    args = {
        "nb": neighbours.T,
        "fl": face_list,
        "v_in": tiles(iterate),
        "jac_in": jacobian.reshape(K, NV, NV, BD, BLK).transpose(1, 2, 3, 0, 4),
        "rhs_in": tiles(right_side),
        "sb_in": self_block.reshape(NV, NV, BD, BLK).transpose(0, 2, 1, 3),
        "dg_in": cell_diag.reshape(NV, BD, BLK).transpose(1, 0, 2),
    }
    field = (NV, BD, T, BLK)
    face = (NV, H, T, BLK)
    small = (NV, H // 4, T, BLK)
    ring = (NV, BD // 4, T, BLK)
    scratch = {
        "v": field,
        "jac": (NV, NV, BD, K, BLK),
        "rhs": field,
        "sb": (NV, BD, NV, BLK),
        "dg": (BD, NV, BLK),
        "pre": field,
        "cf": field,
        "cc": field,
        "corr": field,
        "cpre": field,
        "cd": field,
        "rim_near": face,
        "rim_far": face,
    }
    for name in FINE + SMALL:
        for key in ("face_out_", "near_in_", "far_in_"):
            scratch[key + name] = face if name in FINE else small
    for name in RING:
        for key in ("ring_out_", "ring_in_"):
            scratch[key + name] = ring
    n_sems = 2 * len(FINE + SMALL) + len(RING)
    names = list(args) + ["v_out", "r_out"] + list(scratch) + ["load_sem", "send_sem", "recv_sem"]
    hbm = pl.BlockSpec(memory_space=pltpu.HBM)
    smem = pl.BlockSpec(memory_space=pltpu.SMEM)
    out = pl.pallas_call(
        functools.partial(kernel, n_tm, n_space, names),
        out_shape=(jax.ShapeDtypeStruct(field, jnp.float32),) * 2,
        in_specs=[smem, smem] + [hbm] * 5,
        out_specs=(hbm, hbm),
        scratch_shapes=[pltpu.VMEM(shape, jnp.float32) for shape in scratch.values()]
        + [
            pltpu.SemaphoreType.DMA((7,)),
            pltpu.SemaphoreType.DMA((n_sems,)),
            pltpu.SemaphoreType.DMA((n_sems,)),
        ],
        compiler_params=pltpu.CompilerParams(
            collective_id=0, has_side_effects=True, vmem_limit_bytes=48 * 1024 * 1024
        ),
        name="vcycle",
    )(*args.values())
    return tuple(untile(x) for x in out)


def solution(mesh):
    in_specs = (
        P("tm", None, "space"),
        P("tm", None, "space"),
        P(None, None, None, "space"),
        P(None, None, "space"),
        P(None, "space"),
        P("space", None),
        P("space"),
    )
    out_specs = (P("tm", None, "space"), P("tm", None, "space"))
    step = functools.partial(body, mesh.shape["tm"], mesh.shape["space"])
    return jax.shard_map(step, mesh=mesh, in_specs=in_specs, out_specs=out_specs, check_vma=False)
```

```python
import functools

import jax
import jax.numpy as jnp
from jax import lax
from jax.experimental import pallas as pl
from jax.experimental.pallas import tpu as pltpu
from jax.sharding import PartitionSpec as P

NV = 5
BLK = 128
K = 6
BD = 16
H = 8
T = 8

WEIGHT = 0.5
COARSE = WEIGHT / 4.0
DAMP = 0.7
MESH = pl.DeviceIdType.MESH

FINE = ("f1", "f2", "f3", "f5", "f6")
SMALL = ("c0", "c1", "c2", "c3", "c4")
PARTS = ((0, 2), (2, 2), (4, 1))
RING = ("f1", "f2", "f3", "f5", "f6", "c1", "c2", "c3", "c4")


def roll(x, n):
    return pltpu.roll(x, n % T, axis=0)


def kernel(n_tm, n_space, names, *refs):
    r = dict(zip(names, refs))
    tm = lax.axis_index("tm")
    slab = lax.axis_index("space")
    core = lax.rem(slab, 2)
    near_dev = (tm, slab + 1 - 2 * core)
    far_slab = slab - 1 + 2 * core
    has_far = jnp.logical_and(far_slab >= 0, far_slab < n_space)
    far_dev = (tm, far_slab)
    next_dev = (lax.rem(tm + 1, n_tm), slab)
    prev_dev = (lax.rem(tm + n_tm - 1, n_tm), slab)
    near_slot = 1 - core
    far_slot = core
    nb, fl = r["nb"], r["fl"]
    jac, sb, dg = r["jac"], r["sb"], r["dg"]
    v, pre, rhs = r["v"], r["pre"], r["rhs"]
    cf, cc = r["cf"], r["cc"]
    corr, cpre, cd = r["corr"], r["cpre"], r["cd"]
    late, rank, others = r["late"], r["rank"], r["others"]

    sub = lax.broadcasted_iota(jnp.int32, (T, BLK), 0)
    sub4 = lax.rem(sub, 4)

    barrier = pltpu.get_barrier_semaphore()
    for dev in (near_dev, next_dev, prev_dev):
        pl.semaphore_signal(barrier, inc=1, device_id=dev, device_id_type=MESH)

    @pl.when(has_far)
    def _():
        pl.semaphore_signal(barrier, inc=1, device_id=far_dev, device_id_type=MESH)

    loads = {}
    for i, (src, dst) in enumerate(
        (
            ("fl_in", "fl"),
            ("v_in", "v"),
            ("nb_in", "nb"),
            ("jac_in", "jac"),
            ("rhs_in", "rhs"),
            ("sb_in", "sb"),
            ("dg_in", "dg"),
        )
    ):
        loads[dst] = pltpu.make_async_copy(r[src], r[dst], r["load_sem"].at[i])
        loads[dst].start()

    sem_index = {}
    for name in FINE + SMALL:
        for side in ("near", "far"):
            for part in PARTS if (name, side) == ("f3", "far") else (None,):
                sem_index[name, side, part] = len(sem_index)
    for name in RING:
        for side in ("ring0", "ring1"):
            sem_index[name, side, None] = len(sem_index)

    def copy_of(name, side, part=None):
        i = sem_index[name, side, part]
        if side in ("near", "far"):
            src, dst = r["face_out_" + name], r[side + "_in_" + name]
            dev = near_dev if side == "near" else far_dev
            if part:
                src, dst = src.at[pl.ds(*part)], dst.at[pl.ds(*part)]
        else:
            src, dst = (r["ring_%s_%s_%s" % (way, name, side[-1])] for way in ("out", "in"))
            dev = next_dev
        return pltpu.make_async_remote_copy(
            src_ref=src,
            dst_ref=dst,
            send_sem=r["send_sem"].at[i],
            recv_sem=r["recv_sem"].at[i],
            device_id=dev,
            device_id_type=MESH,
        )

    def send_far(name, part=None):
        @pl.when(has_far)
        def _():
            copy_of(name, "far", part).start()

    def send_faces(name):
        send_far(name)
        copy_of(name, "near").start()

    def wait(name, side):
        if side == "far":

            @pl.when(has_far)
            def _():
                for part in PARTS if name == "f3" else (None,):
                    copy_of(name, side, part).wait_recv()

        else:
            copy_of(name, side).wait_recv()

    def row(ref, idx, k):
        return ref[idx + (pl.ds(k, T, stride=0), slice(None))]

    def own_block(b, x, g, field, three_w, timed):
        acc = []
        for a in range(NV):
            t = g[a] - (row(dg, (b,), a) + three_w) * x[a]
            t = t + timed(x[a])
            for j in range(NV):
                if j != a:
                    t = t - row(sb, (a, b), j) * x[j]
            acc.append(t)
        for k in range(2, K):
            at = nb[k, b]
            p = [field[j, at] for j in range(NV)]
            for a in range(NV):
                for j in range(NV):
                    acc[a] = acc[a] - row(jac, (a, j, b), k) * p[j]
        return acc

    def timed_fine(x):
        zero = jnp.zeros_like(x)
        one = jnp.where(sub >= 1, roll(x, 1), zero)
        two = jnp.where(sub >= 2, roll(x, 2), zero)
        return (4.0 * WEIGHT) * one - WEIGHT * two

    def timed_coarse(x):
        return (4.0 * COARSE) * jnp.where(sub >= 4, roll(x, 4), jnp.zeros_like(x))

    def grouped(count, values_of, keep, width):
        def step(g, carry):
            at = [width * g + i for i in range(width)]
            got = [values_of(b) for b in at]
            for b, values in zip(at, got):
                keep(b, values)
            return carry

        lax.fori_loop(0, count // width, step, 0)

    def store(ref, b, values):
        for a in range(NV):
            ref[a, b] = values[a]

    def own(field, g, out, three_w, timed):
        def values_of(b):
            x = [field[j, b] for j in range(NV)]
            return own_block(b, x, [g[a, b] for a in range(NV)], field, three_w, timed)

        grouped(BD, values_of, functools.partial(store, out), 2)

    def rim(acc, b, field, slot):
        at = jnp.bitwise_and(nb[slot, b], H - 1)
        p = [field[j, at] for j in range(NV)]
        for a in range(NV):
            for j in range(NV):
                acc[a] = acc[a] - row(jac, (a, j, b), slot) * p[j]
        return acc

    def fold_rim(out, field, slot):
        def values_of(b):
            return rim([out[a, b] for a in range(NV)], b, field, slot)

        grouped(BD, values_of, functools.partial(store, out), 4)

    def place_fine(x, i):
        q = WEIGHT * (roll(x, 2) - jnp.where(sub == 0, 4.0 * roll(x, 1), jnp.zeros_like(x)))
        return roll(q, 2 * i) if i else q

    def place_coarse(x, i):
        return COARSE * jnp.where(sub >= 4, x, x - 4.0 * roll(x, 4))

    def ring_tile(four, place):
        tile = place(four[0], 0)
        for i in range(1, 4):
            mine = lax.div(sub, 2) == i if place is place_fine else sub4 == i
            tile = jnp.where(mine, place(four[i], i), tile)
        return tile

    def send_others(name, field, place):
        out = r["ring_out_" + name + "_1"]
        for g in range(2):
            got = [[field[a, others[4 * g + i]] for i in range(4)] for a in range(NV)]
            for a in range(NV):
                out[a, g] = ring_tile(got[a], place)
        copy_of(name, "ring1").start()

    def spread(turns, i):
        x = turns[-i]
        for u in range(1, 4):
            x = jnp.where(sub4 == u, turns[u - i], x)
        return x

    def turns_of(tile):
        return {d: (roll(tile, d) if d else tile) for d in range(-3, 4)}

    def open_ring(name, part, fine):
        wait(name, "ring%d" % part)
        src = r["ring_in_%s_%d" % (name, part)]

        def body(a, carry):
            got = []
            for g in range(2):
                tile = src[a, g]
                turns = None if fine else turns_of(tile)
                for i in range(4):
                    if fine:
                        q = roll(tile, T - 2 * i) if i else tile
                        got.append(jnp.where(sub < 2, q, jnp.zeros_like(q)))
                    else:
                        got.append(spread(turns, i))
            for i in range(H):
                late[a, H * part + i] = got[i]
            return carry

        lax.fori_loop(0, NV, body, 0)

    def unpack(name, side):
        wait(name, side)
        src, out = r[side + "_in_" + name], r["rim_" + side]

        def body(a, carry):
            got = []
            for g in range(H // 4):
                turns = turns_of(src[a, g])
                got += [spread(turns, i) for i in range(4)]
            for i in range(H):
                out[a, i] = got[i]
            return carry

        lax.fori_loop(0, NV, body, 0)
        return out

    def mean4(x):
        x = x + jnp.where(lax.rem(sub, 2) == 0, roll(x, -1), roll(x, 1))
        x = x + jnp.where(sub4 < 2, roll(x, -2), roll(x, 2))
        return 0.25 * x

    def faces(value_of, place, ring_name, full=None, small=None, average=False):
        kept = r["face_out_" + full] if full else r["face_kept"]
        for g in range(2):
            got = [value_of(4 * g + i) for i in range(4)]
            for a in range(NV):
                for i in range(4):
                    kept[a, 4 * g + i] = got[i][a]
                if small:
                    four = [mean4(x[a]) if average else x[a] for x in got]
                    tile = four[0]
                    for i in range(1, 4):
                        tile = jnp.where(sub4 == i, four[i], tile)
                    r["face_out_" + small][a, g] = tile
        send_faces(small or full)
        for g in range(2):
            for a in range(NV):
                four = [kept[a, 4 * g + i] for i in range(4)]
                r["ring_out_" + ring_name + "_0"][a, g] = ring_tile(four, place)
        copy_of(ring_name, "ring0").start()

    def swept_face(field, p, scale, far, h):
        b = fl[h]
        acc = rim([p[a, b] - late[a, h] for a in range(NV)], b, far, far_slot)
        return [field[a, b] + scale[a, b] * acc[a] for a in range(NV)]

    def swept(field, p, scale, far, b):
        at = rank[b]
        acc = rim([p[a, b] - late[a, at] for a in range(NV)], b, far, far_slot)
        return [field[a, b] + scale[a, b] * acc[a] for a in range(NV)]

    def sweep(field, p, scale, far):
        grouped(BD, functools.partial(swept, field, p, scale, far), functools.partial(store, field), 4)

    @pl.when(jnp.logical_not(has_far))
    def _():
        for name in FINE + SMALL:
            ref = r["far_in_" + name]

            def clear(a, carry, ref=ref):
                for i in range(ref.shape[1]):
                    ref[a, i] = jnp.zeros((T, BLK), jnp.float32)
                return carry

            lax.fori_loop(0, NV, clear, 0)

    loads["fl"].wait()
    loads["v"].wait()
    pl.semaphore_wait(barrier, jnp.where(has_far, 4, 3))
    faces(lambda h: [v[a, fl[h]] for a in range(NV)], place_fine, "f1", full="f1")

    def rank_of(b, count):
        at = jnp.minimum(H + count, BD - 1)
        for h in range(H):
            at = jnp.where(fl[h] == b, h, at)
        rank[b] = at
        return jnp.where(at >= H, count + 1, count)

    lax.fori_loop(0, BD, rank_of, jnp.int32(0))

    def other_of(i, carry):
        b = jnp.int32(0)
        for c in range(BD):
            b = jnp.where(rank[c] == H + i, c, b)
        others[i] = b
        return carry

    lax.fori_loop(0, H, other_of, 0)
    send_others("f1", v, place_fine)
    for name in ("nb", "jac", "rhs", "sb", "dg"):
        loads[name].wait()

    def scales(b):
        d = [row(dg, (b,), a) for a in range(NV)]
        return [DAMP / (3.0 * WEIGHT + x) for x in d] + [DAMP / (3.0 * COARSE + x) for x in d]

    def keep_scales(b, values):
        store(cf, b, values[:NV])
        store(cc, b, values[NV:])

    grouped(BD, scales, keep_scales, 2)

    def arrive(name, out):
        wait(name, "near")
        fold_rim(out, r["near_in_" + name], near_slot)
        open_ring(name, 0, True)
        wait(name, "far")
        return r["far_in_" + name]

    own(v, rhs, pre, 3.0 * WEIGHT, timed_fine)
    far = arrive("f1", pre)
    faces(functools.partial(swept_face, v, pre, cf, far), place_fine, "f2", full="f2")
    open_ring("f1", 1, True)
    sweep(v, pre, cf, far)
    send_others("f2", v, place_fine)
    own(v, rhs, pre, 3.0 * WEIGHT, timed_fine)
    far = arrive("f2", pre)
    faces(functools.partial(swept_face, v, pre, cf, far), place_fine, "f3", full="f3", small="c0", average=True)
    open_ring("f2", 1, True)
    sweep(v, pre, cf, far)
    send_others("f3", v, place_fine)
    send_far("f3", PARTS[0])
    copy_of("f3", "near").start()

    own(v, rhs, pre, 3.0 * WEIGHT, timed_fine)
    grouped(BD, lambda b: [mean4(pre[a, b]) for a in range(NV)], functools.partial(store, cpre), 2)
    fold_rim(cpre, unpack("c0", "near"), near_slot)
    open_ring("f3", 0, True)
    far = unpack("c0", "far")

    def first_face(h):
        b = fl[h]
        acc = rim([cpre[a, b] - mean4(late[a, h]) for a in range(NV)], b, far, far_slot)
        return [cc[a, b] * acc[a] for a in range(NV)]

    def first(b):
        q = [late[a, rank[b]] for a in range(NV)]
        acc = rim([cpre[a, b] - mean4(q[a]) for a in range(NV)], b, far, far_slot)
        return acc + [cc[a, b] * acc[a] for a in range(NV)] + [pre[a, b] - q[a] for a in range(NV)]

    def keep_first(b, values):
        store(cd, b, values[:NV])
        store(corr, b, values[NV : 2 * NV])
        store(pre, b, values[2 * NV :])

    faces(first_face, place_coarse, "c1", small="c1")
    open_ring("f3", 1, True)
    grouped(BD, first, keep_first, 2)
    send_others("c1", corr, place_coarse)
    send_far("f3", PARTS[1])

    for name, later in (("c1", "c2"), ("c2", "c3"), ("c3", "c4")):
        place = place_fine if later == "c4" else place_coarse
        own(corr, cd, cpre, 3.0 * COARSE, timed_coarse)
        fold_rim(cpre, unpack(name, "near"), near_slot)
        open_ring(name, 0, False)
        if name == "c3":
            for side, slot in (("near", near_slot), ("far", far_slot)):
                wait("f3", side)
                fold_rim(pre, r[side + "_in_f3"], slot)
        far = unpack(name, "far")
        faces(functools.partial(swept_face, corr, cpre, cc, far), place, later, small=later)
        open_ring(name, 1, False)
        sweep(corr, cpre, cc, far)
        send_others(later, corr, place)
        if later == "c2":
            send_far("f3", PARTS[2])

    own(corr, pre, pre, 3.0 * WEIGHT, timed_fine)
    grouped(BD, lambda b: [v[a, b] + corr[a, b] for a in range(NV)], functools.partial(store, v), 4)
    fold_rim(pre, unpack("c4", "near"), near_slot)
    open_ring("c4", 0, True)
    far = unpack("c4", "far")
    for name, later in (("c4", "f5"), ("f5", "f6")):
        faces(functools.partial(swept_face, v, pre, cf, far), place_fine, later, full=later)
        open_ring(name, 1, True)
        sweep(v, pre, cf, far)
        send_others(later, v, place_fine)
        if later == "f6":
            save_v = pltpu.make_async_copy(v, r["v_out"], r["load_sem"].at[7])
            save_v.start()
        own(v, rhs, pre, 3.0 * WEIGHT, timed_fine)
        far = arrive(later, pre)
    open_ring("f6", 1, True)

    def last(b):
        at = rank[b]
        return rim([pre[a, b] - late[a, at] for a in range(NV)], b, far, far_slot)

    grouped(BD, last, functools.partial(store, pre), 4)
    save_r = pltpu.make_async_copy(pre, r["r_out"], r["load_sem"].at[8])
    save_r.start()
    for key in sem_index:
        if key[1] == "far":

            @pl.when(has_far)
            def _(key=key):
                copy_of(*key).wait_send()

        else:
            copy_of(*key).wait_send()
    save_v.wait()
    save_r.wait()


def finish(*refs):
    ins, outs, bufs, sems = refs[:2], refs[2:4], refs[4:6], refs[6]
    parts = []
    for i in range(2):
        for a in range(NV):
            parts.append(
                (
                    pltpu.make_async_copy(ins[i].at[a], bufs[i].at[a], sems.at[0, i, a]),
                    pltpu.make_async_copy(bufs[i].at[a], outs[i].at[a], sems.at[1, i, a]),
                )
            )
    for get, _ in parts:
        get.start()
    for get, put in parts:
        get.wait()
        put.start()
    for _, put in parts:
        put.wait()


def body(n_tm, n_space, iterate, right_side, jacobian, self_block, cell_diag, neighbours, face_list):
    def tiles(x):
        return x.reshape(T, NV, BD, BLK).transpose(1, 2, 0, 3)

    def untile(x):
        return x.transpose(2, 0, 1, 3).reshape(T, NV, BD * BLK)

    args = {
        "nb_in": neighbours.T,
        "fl_in": face_list,
        "v_in": tiles(iterate),
        "jac_in": jacobian.reshape(K, NV, NV, BD, BLK).transpose(1, 2, 3, 0, 4),
        "rhs_in": tiles(right_side),
        "sb_in": self_block.reshape(NV, NV, BD, BLK).transpose(0, 2, 1, 3),
        "dg_in": cell_diag.reshape(NV, BD, BLK).transpose(1, 0, 2),
    }
    field = (NV, BD, T, BLK)
    face = (NV, H, T, BLK)
    small = (NV, H // 4, T, BLK)
    scratch = {
        "v": field,
        "jac": (NV, NV, BD, K, BLK),
        "rhs": field,
        "sb": (NV, BD, NV, BLK),
        "dg": (BD, NV, BLK),
        "pre": field,
        "cf": field,
        "cc": field,
        "corr": field,
        "cpre": field,
        "cd": field,
        "late": field,
        "face_kept": face,
        "rim_near": face,
        "rim_far": face,
    }
    for name in FINE + SMALL:
        for key in ("face_out_", "near_in_", "far_in_"):
            scratch[key + name] = face if name in FINE else small
    for name in RING:
        for key in ("ring_out_", "ring_in_"):
            for part in ("_0", "_1"):
                scratch[key + name + part] = small
    n_sems = 2 * len(FINE + SMALL) + len(PARTS) - 1 + 2 * len(RING)
    names = list(args) + ["v_out", "r_out"] + list(scratch) + ["fl", "nb", "rank", "others", "load_sem", "send_sem", "recv_sem"]
    hbm = pl.BlockSpec(memory_space=pltpu.HBM)
    out = pl.pallas_call(
        functools.partial(kernel, n_tm, n_space, names),
        out_shape=(jax.ShapeDtypeStruct(field, jnp.float32),) * 2,
        in_specs=[hbm] * 7,
        out_specs=(hbm, hbm),
        scratch_shapes=[pltpu.VMEM(shape, jnp.float32) for shape in scratch.values()]
        + [
            pltpu.SMEM((H,), jnp.int32),
            pltpu.SMEM((K, BD), jnp.int32),
            pltpu.SMEM((BD,), jnp.int32),
            pltpu.SMEM((H,), jnp.int32),
            pltpu.SemaphoreType.DMA((9,)),
            pltpu.SemaphoreType.DMA((n_sems,)),
            pltpu.SemaphoreType.DMA((n_sems,)),
        ],
        compiler_params=pltpu.CompilerParams(
            collective_id=0, has_side_effects=True, vmem_limit_bytes=62 * 1024 * 1024
        ),
        name="vcycle",
    )(*args.values())
    out = pl.pallas_call(
        finish,
        out_shape=(jax.ShapeDtypeStruct(field, jnp.float32),) * 2,
        in_specs=[hbm] * 2,
        out_specs=(hbm, hbm),
        scratch_shapes=[pltpu.VMEM(field, jnp.float32)] * 2 + [pltpu.SemaphoreType.DMA((2, 2, NV))],
        compiler_params=pltpu.CompilerParams(vmem_limit_bytes=62 * 1024 * 1024),
        name="finish",
    )(*out)
    return tuple(untile(x) for x in out)


def solution(mesh):
    in_specs = (
        P("tm", None, "space"),
        P("tm", None, "space"),
        P(None, None, None, "space"),
        P(None, None, "space"),
        P(None, "space"),
        P("space", None),
        P("space"),
    )
    out_specs = (P("tm", None, "space"), P("tm", None, "space"))
    step = functools.partial(body, mesh.shape["tm"], mesh.shape["space"])
    return jax.shard_map(step, mesh=mesh, in_specs=in_specs, out_specs=out_specs, check_vma=False)
```

```python
import functools

import jax
import jax.numpy as jnp
from jax import lax
from jax.experimental import pallas as pl
from jax.experimental.pallas import tpu as pltpu
from jax.sharding import PartitionSpec as P

NV = 5
BLK = 128
K = 6
BD = 16
H = 8
T = 8

WEIGHT = 0.5
COARSE = WEIGHT / 4.0
DAMP = 0.7
MESH = pl.DeviceIdType.MESH

FINE = ("f1", "f2", "f3", "f5", "f6")
SMALL = ("c0", "c1", "c2", "c3", "c4")
PARTS = ((0, 2), (2, 2), (4, 1))
RING = ("f1", "f2", "f3", "f5", "f6", "c1", "c2", "c3", "c4")


def roll(x, n):
    return pltpu.roll(x, n % T, axis=0)


def kernel(n_tm, n_space, names, *refs):
    r = dict(zip(names, refs))
    tm = lax.axis_index("tm")
    slab = lax.axis_index("space")
    core = lax.rem(slab, 2)
    near_dev = (tm, slab + 1 - 2 * core)
    far_slab = slab - 1 + 2 * core
    has_far = jnp.logical_and(far_slab >= 0, far_slab < n_space)
    far_dev = (tm, far_slab)
    next_dev = (lax.rem(tm + 1, n_tm), slab)
    prev_dev = (lax.rem(tm + n_tm - 1, n_tm), slab)
    near_slot = 1 - core
    far_slot = core
    nb, fl = r["nb"], r["fl"]
    jac, sb, dg = r["jac"], r["sb"], r["dg"]
    v, pre, rhs = r["v"], r["pre"], r["rhs"]
    cf, cc = r["cf"], r["cc"]
    corr, cpre, cd = r["corr"], r["cpre"], r["cd"]
    late, rank, others = r["late"], r["rank"], r["others"]
    base, aim, jf, jc = r["base"], r["aim"], r["jf"], r["jc"]

    sub = lax.broadcasted_iota(jnp.int32, (T, BLK), 0)
    sub4 = lax.rem(sub, 4)

    barrier = pltpu.get_barrier_semaphore()
    for dev in (near_dev, next_dev, prev_dev):
        pl.semaphore_signal(barrier, inc=1, device_id=dev, device_id_type=MESH)

    @pl.when(has_far)
    def _():
        pl.semaphore_signal(barrier, inc=1, device_id=far_dev, device_id_type=MESH)

    loads = {}
    for i, (src, dst) in enumerate(
        (
            ("fl_in", "fl"),
            ("v_in", "v"),
            ("nb_in", "nb"),
            ("jac_in", "jac"),
            ("rhs_in", "rhs"),
            ("sb_in", "sb"),
            ("dg_in", "dg"),
        )
    ):
        loads[dst] = pltpu.make_async_copy(r[src], r[dst], r["load_sem"].at[i])
        loads[dst].start()

    sem_index = {}
    for name in FINE + SMALL:
        for side in ("near", "far"):
            for part in PARTS if (name, side) == ("f3", "far") else (None,):
                sem_index[name, side, part] = len(sem_index)
    for name in RING:
        for side in ("ring0", "ring1"):
            sem_index[name, side, None] = len(sem_index)

    def copy_of(name, side, part=None):
        i = sem_index[name, side, part]
        if side in ("near", "far"):
            src, dst = r["face_out_" + name], r[side + "_in_" + name]
            dev = near_dev if side == "near" else far_dev
            if part:
                src, dst = src.at[pl.ds(*part)], dst.at[pl.ds(*part)]
        else:
            src, dst = (r["ring_%s_%s_%s" % (way, name, side[-1])] for way in ("out", "in"))
            dev = next_dev
        return pltpu.make_async_remote_copy(
            src_ref=src,
            dst_ref=dst,
            send_sem=r["send_sem"].at[i],
            recv_sem=r["recv_sem"].at[i],
            device_id=dev,
            device_id_type=MESH,
        )

    def send_far(name, part=None):
        @pl.when(has_far)
        def _():
            copy_of(name, "far", part).start()

    def send_faces(name):
        send_far(name)
        copy_of(name, "near").start()

    def wait(name, side):
        if side == "far":

            @pl.when(has_far)
            def _():
                for part in PARTS if name == "f3" else (None,):
                    copy_of(name, side, part).wait_recv()

        else:
            copy_of(name, side).wait_recv()

    def row(ref, idx, k):
        return ref[idx + (pl.ds(k, T, stride=0), slice(None))]

    def own_block(b, x, g, field, three_w, timed):
        acc = []
        for a in range(NV):
            t = g[a] - (row(dg, (b,), a) + three_w) * x[a]
            t = t + timed(x[a])
            for j in range(NV):
                if j != a:
                    t = t - row(sb, (a, b), j) * x[j]
            acc.append(t)
        for k in range(2, K):
            at = nb[k, b]
            p = [field[j, at] for j in range(NV)]
            for a in range(NV):
                for j in range(NV):
                    acc[a] = acc[a] - row(jac, (a, j, b), k) * p[j]
        return acc

    def timed_fine(x):
        zero = jnp.zeros_like(x)
        one = jnp.where(sub >= 1, roll(x, 1), zero)
        two = jnp.where(sub >= 2, roll(x, 2), zero)
        return (4.0 * WEIGHT) * one - WEIGHT * two

    def timed_coarse(x):
        return (4.0 * COARSE) * jnp.where(sub >= 4, roll(x, 4), jnp.zeros_like(x))

    def grouped(count, values_of, keep, width):
        def step(g, carry):
            at = [width * g + i for i in range(width)]
            got = [values_of(b) for b in at]
            for b, values in zip(at, got):
                keep(b, values)
            return carry

        lax.fori_loop(0, count // width, step, 0)

    def store(ref, b, values):
        for a in range(NV):
            ref[a, b] = values[a]

    def own(field, g, out, three_w, timed):
        def values_of(b):
            x = [field[j, b] for j in range(NV)]
            return own_block(b, x, [g[a, b] for a in range(NV)], field, three_w, timed)

        grouped(BD, values_of, functools.partial(store, out), 2)

    def rim(acc, b, field, slot):
        at = jnp.bitwise_and(nb[slot, b], H - 1)
        p = [field[j, at] for j in range(NV)]
        for a in range(NV):
            for j in range(NV):
                acc[a] = acc[a] - row(jac, (a, j, b), slot) * p[j]
        return acc

    def fold_rim(out, field, slot):
        def values_of(b):
            return rim([out[a, b] for a in range(NV)], b, field, slot)

        grouped(BD, values_of, functools.partial(store, out), 4)

    def place_fine(x, i):
        q = WEIGHT * (roll(x, 2) - jnp.where(sub == 0, 4.0 * roll(x, 1), jnp.zeros_like(x)))
        return roll(q, 2 * i) if i else q

    def place_coarse(x, i):
        return COARSE * jnp.where(sub >= 4, x, x - 4.0 * roll(x, 4))

    def ring_tile(four, place):
        tile = place(four[0], 0)
        for i in range(1, 4):
            mine = lax.div(sub, 2) == i if place is place_fine else sub4 == i
            tile = jnp.where(mine, place(four[i], i), tile)
        return tile

    def send_others(name, field, place):
        out = r["ring_out_" + name + "_1"]
        for g in range(2):
            got = [[field[a, others[4 * g + i]] for i in range(4)] for a in range(NV)]
            for a in range(NV):
                out[a, g] = ring_tile(got[a], place)
        copy_of(name, "ring1").start()

    def spread(turns, i):
        x = turns[-i]
        for u in range(1, 4):
            x = jnp.where(sub4 == u, turns[u - i], x)
        return x

    def turns_of(tile):
        return {d: (roll(tile, d) if d else tile) for d in range(-3, 4)}

    def open_ring(name, part, fine):
        wait(name, "ring%d" % part)
        src = r["ring_in_%s_%d" % (name, part)]

        def body(a, carry):
            got = []
            for g in range(2):
                tile = src[a, g]
                turns = None if fine else turns_of(tile)
                for i in range(4):
                    if fine:
                        q = roll(tile, T - 2 * i) if i else tile
                        got.append(jnp.where(sub < 2, q, jnp.zeros_like(q)))
                    else:
                        got.append(spread(turns, i))
            for i in range(H):
                late[a, H * part + i] = got[i]
            return carry

        lax.fori_loop(0, NV, body, 0)

    def unpack(name, side):
        wait(name, side)
        src, out = r[side + "_in_" + name], r["rim_" + side]

        def body(a, carry):
            got = []
            for g in range(H // 4):
                turns = turns_of(src[a, g])
                got += [spread(turns, i) for i in range(4)]
            for i in range(H):
                out[a, i] = got[i]
            return carry

        lax.fori_loop(0, NV, body, 0)
        return out

    def mean4(x):
        x = x + jnp.where(lax.rem(sub, 2) == 0, roll(x, -1), roll(x, 1))
        x = x + jnp.where(sub4 < 2, roll(x, -2), roll(x, 2))
        return 0.25 * x

    def faces(value_of, place, ring_name, full=None, small=None, average=False):
        kept = r["face_out_" + full] if full else r["face_kept"]
        for g in range(2):
            got = [value_of(4 * g + i) for i in range(4)]
            for a in range(NV):
                for i in range(4):
                    kept[a, 4 * g + i] = got[i][a]
                if small:
                    four = [mean4(x[a]) if average else x[a] for x in got]
                    tile = four[0]
                    for i in range(1, 4):
                        tile = jnp.where(sub4 == i, four[i], tile)
                    r["face_out_" + small][a, g] = tile
        send_faces(small or full)
        for g in range(2):
            for a in range(NV):
                four = [kept[a, 4 * g + i] for i in range(4)]
                r["ring_out_" + ring_name + "_0"][a, g] = ring_tile(four, place)
        copy_of(ring_name, "ring0").start()

    def prepare(values_of):
        def step(g, carry):
            at = [2 * g, 2 * g + 1]
            got = [values_of(h, fl[h]) for h in at]
            for h, values in zip(at, got):
                store(base, h, values)
            return carry

        lax.fori_loop(0, H // 2, step, 0)

    def prepare_sweep(field, p, scale):
        def values_of(h, b):
            return [field[a, b] + scale[a, b] * (p[a, b] - late[a, h]) for a in range(NV)]

        prepare(values_of)

    def face_value(table, far, h):
        at = aim[h]
        p = [far[j, at] for j in range(NV)]
        values = []
        for a in range(NV):
            q = [table[h, NV * a + j] * p[j] for j in range(NV)]
            values.append(base[a, h] - ((q[0] + q[1]) + (q[2] + q[3]) + q[4]))
        return values

    def swept(field, p, scale, far, b):
        at = rank[b]
        acc = rim([p[a, b] - late[a, at] for a in range(NV)], b, far, far_slot)
        return [field[a, b] + scale[a, b] * acc[a] for a in range(NV)]

    def sweep(field, p, scale, far):
        grouped(BD, functools.partial(swept, field, p, scale, far), functools.partial(store, field), 4)

    @pl.when(jnp.logical_not(has_far))
    def _():
        for name in FINE + SMALL:
            ref = r["far_in_" + name]

            def clear(a, carry, ref=ref):
                for i in range(ref.shape[1]):
                    ref[a, i] = jnp.zeros((T, BLK), jnp.float32)
                return carry

            lax.fori_loop(0, NV, clear, 0)

    loads["fl"].wait()
    loads["v"].wait()
    pl.semaphore_wait(barrier, jnp.where(has_far, 4, 3))
    faces(lambda h: [v[a, fl[h]] for a in range(NV)], place_fine, "f1", full="f1")

    def rank_of(b, count):
        at = jnp.minimum(H + count, BD - 1)
        for h in range(H):
            at = jnp.where(fl[h] == b, h, at)
        rank[b] = at
        return jnp.where(at >= H, count + 1, count)

    lax.fori_loop(0, BD, rank_of, jnp.int32(0))

    def other_of(i, carry):
        b = jnp.int32(0)
        for c in range(BD):
            b = jnp.where(rank[c] == H + i, c, b)
        others[i] = b
        return carry

    lax.fori_loop(0, H, other_of, 0)
    send_others("f1", v, place_fine)
    for name in ("nb", "jac", "rhs", "sb", "dg"):
        loads[name].wait()

    def scales(b):
        d = [row(dg, (b,), a) for a in range(NV)]
        return [DAMP / (3.0 * WEIGHT + x) for x in d] + [DAMP / (3.0 * COARSE + x) for x in d]

    def keep_scales(b, values):
        store(cf, b, values[:NV])
        store(cc, b, values[NV:])

    grouped(BD, scales, keep_scales, 2)

    def scaled(h, carry):
        b = fl[h]
        aim[h] = jnp.bitwise_and(nb[far_slot, b], H - 1)
        for a in range(NV):
            fine, coarse = cf[a, b], cc[a, b]
            x = [row(jac, (a, j, b), far_slot) for j in range(NV)]
            for j in range(NV):
                jf[h, NV * a + j] = fine * x[j]
                jc[h, NV * a + j] = coarse * x[j]
        return carry

    lax.fori_loop(0, H, scaled, 0)

    def arrive(name, out):
        wait(name, "near")
        fold_rim(out, r["near_in_" + name], near_slot)
        open_ring(name, 0, True)
        prepare_sweep(v, out, cf)
        wait(name, "far")
        return r["far_in_" + name]

    own(v, rhs, pre, 3.0 * WEIGHT, timed_fine)
    far = arrive("f1", pre)
    faces(functools.partial(face_value, jf, far), place_fine, "f2", full="f2")
    open_ring("f1", 1, True)
    sweep(v, pre, cf, far)
    send_others("f2", v, place_fine)
    own(v, rhs, pre, 3.0 * WEIGHT, timed_fine)
    far = arrive("f2", pre)
    faces(functools.partial(face_value, jf, far), place_fine, "f3", full="f3", small="c0", average=True)
    open_ring("f2", 1, True)
    sweep(v, pre, cf, far)
    send_others("f3", v, place_fine)
    send_far("f3", PARTS[0])
    copy_of("f3", "near").start()

    own(v, rhs, pre, 3.0 * WEIGHT, timed_fine)
    grouped(BD, lambda b: [mean4(pre[a, b]) for a in range(NV)], functools.partial(store, cpre), 2)
    fold_rim(cpre, unpack("c0", "near"), near_slot)
    open_ring("f3", 0, True)
    prepare(lambda h, b: [cc[a, b] * (cpre[a, b] - mean4(late[a, h])) for a in range(NV)])
    far = unpack("c0", "far")

    def first(b):
        q = [late[a, rank[b]] for a in range(NV)]
        acc = rim([cpre[a, b] - mean4(q[a]) for a in range(NV)], b, far, far_slot)
        return acc + [cc[a, b] * acc[a] for a in range(NV)] + [pre[a, b] - q[a] for a in range(NV)]

    def keep_first(b, values):
        store(cd, b, values[:NV])
        store(corr, b, values[NV : 2 * NV])
        store(pre, b, values[2 * NV :])

    faces(functools.partial(face_value, jc, far), place_coarse, "c1", small="c1")
    open_ring("f3", 1, True)
    grouped(BD, first, keep_first, 2)
    send_others("c1", corr, place_coarse)
    send_far("f3", PARTS[1])

    for name, later in (("c1", "c2"), ("c2", "c3"), ("c3", "c4")):
        place = place_fine if later == "c4" else place_coarse
        own(corr, cd, cpre, 3.0 * COARSE, timed_coarse)
        fold_rim(cpre, unpack(name, "near"), near_slot)
        open_ring(name, 0, False)
        if name == "c3":
            for side, slot in (("near", near_slot), ("far", far_slot)):
                wait("f3", side)
                fold_rim(pre, r[side + "_in_f3"], slot)
        prepare_sweep(corr, cpre, cc)
        far = unpack(name, "far")
        faces(functools.partial(face_value, jc, far), place, later, small=later)
        open_ring(name, 1, False)
        sweep(corr, cpre, cc, far)
        send_others(later, corr, place)
        if later == "c2":
            send_far("f3", PARTS[2])

    own(corr, pre, pre, 3.0 * WEIGHT, timed_fine)
    grouped(BD, lambda b: [v[a, b] + corr[a, b] for a in range(NV)], functools.partial(store, v), 4)
    fold_rim(pre, unpack("c4", "near"), near_slot)
    open_ring("c4", 0, True)
    prepare_sweep(v, pre, cf)
    far = unpack("c4", "far")
    for name, later in (("c4", "f5"), ("f5", "f6")):
        faces(functools.partial(face_value, jf, far), place_fine, later, full=later)
        open_ring(name, 1, True)
        sweep(v, pre, cf, far)
        send_others(later, v, place_fine)
        if later == "f6":
            save_v = pltpu.make_async_copy(v, r["v_out"], r["load_sem"].at[7])
            save_v.start()
        own(v, rhs, pre, 3.0 * WEIGHT, timed_fine)
        if later == "f5":
            far = arrive(later, pre)
    wait("f6", "near")
    fold_rim(pre, r["near_in_f6"], near_slot)
    open_ring("f6", 0, True)
    open_ring("f6", 1, True)
    grouped(
        BD,
        lambda b: [pre[a, b] - late[a, rank[b]] for a in range(NV)],
        functools.partial(store, pre),
        4,
    )
    wait("f6", "far")
    save_r = []
    for g in range(4):
        at = [4 * g + i for i in range(4)]
        got = [rim([pre[a, b] for a in range(NV)], b, r["far_in_f6"], far_slot) for b in at]
        for b, values in zip(at, got):
            store(pre, b, values)
        quarter = (slice(None), pl.ds(4 * g, 4))
        save_r.append(
            pltpu.make_async_copy(pre.at[quarter], r["r_out"].at[quarter], r["load_sem"].at[8 + g])
        )
        save_r[-1].start()
    for key in sem_index:
        if key[1] == "far":

            @pl.when(has_far)
            def _(key=key):
                copy_of(*key).wait_send()

        else:
            copy_of(*key).wait_send()
    save_v.wait()
    for save in save_r:
        save.wait()


def finish(*refs):
    ins, outs, bufs, sems = refs[:2], refs[2:4], refs[4:6], refs[6]
    parts = []
    for i in range(2):
        for a in range(NV):
            parts.append(
                (
                    pltpu.make_async_copy(ins[i].at[a], bufs[i].at[a], sems.at[0, i, a]),
                    pltpu.make_async_copy(bufs[i].at[a], outs[i].at[a], sems.at[1, i, a]),
                )
            )
    for get, _ in parts:
        get.start()
    for get, put in parts:
        get.wait()
        put.start()
    for _, put in parts:
        put.wait()


def body(n_tm, n_space, iterate, right_side, jacobian, self_block, cell_diag, neighbours, face_list):
    def tiles(x):
        return x.reshape(T, NV, BD, BLK).transpose(1, 2, 0, 3)

    def untile(x):
        return x.transpose(2, 0, 1, 3).reshape(T, NV, BD * BLK)

    args = {
        "nb_in": neighbours.T,
        "fl_in": face_list,
        "v_in": tiles(iterate),
        "jac_in": jacobian.reshape(K, NV, NV, BD, BLK).transpose(1, 2, 3, 0, 4),
        "rhs_in": tiles(right_side),
        "sb_in": self_block.reshape(NV, NV, BD, BLK).transpose(0, 2, 1, 3),
        "dg_in": cell_diag.reshape(NV, BD, BLK).transpose(1, 0, 2),
    }
    field = (NV, BD, T, BLK)
    face = (NV, H, T, BLK)
    small = (NV, H // 4, T, BLK)
    scratch = {
        "v": field,
        "jac": (NV, NV, BD, K, BLK),
        "rhs": field,
        "sb": (NV, BD, NV, BLK),
        "dg": (BD, NV, BLK),
        "pre": field,
        "cf": field,
        "cc": field,
        "corr": field,
        "cpre": field,
        "cd": field,
        "late": field,
        "face_kept": face,
        "base": face,
        "jf": (H, NV * NV, T, BLK),
        "jc": (H, NV * NV, T, BLK),
        "rim_near": face,
        "rim_far": face,
    }
    for name in FINE + SMALL:
        for key in ("face_out_", "near_in_", "far_in_"):
            scratch[key + name] = face if name in FINE else small
    for name in RING:
        for key in ("ring_out_", "ring_in_"):
            for part in ("_0", "_1"):
                scratch[key + name + part] = small
    n_sems = 2 * len(FINE + SMALL) + len(PARTS) - 1 + 2 * len(RING)
    names = list(args) + ["v_out", "r_out"] + list(scratch) + ["fl", "nb", "aim", "rank", "others", "load_sem", "send_sem", "recv_sem"]
    hbm = pl.BlockSpec(memory_space=pltpu.HBM)
    out = pl.pallas_call(
        functools.partial(kernel, n_tm, n_space, names),
        out_shape=(jax.ShapeDtypeStruct(field, jnp.float32),) * 2,
        in_specs=[hbm] * 7,
        out_specs=(hbm, hbm),
        scratch_shapes=[pltpu.VMEM(shape, jnp.float32) for shape in scratch.values()]
        + [
            pltpu.SMEM((H,), jnp.int32),
            pltpu.SMEM((K, BD), jnp.int32),
            pltpu.SMEM((H,), jnp.int32),
            pltpu.SMEM((BD,), jnp.int32),
            pltpu.SMEM((H,), jnp.int32),
            pltpu.SemaphoreType.DMA((12,)),
            pltpu.SemaphoreType.DMA((n_sems,)),
            pltpu.SemaphoreType.DMA((n_sems,)),
        ],
        compiler_params=pltpu.CompilerParams(
            collective_id=0, has_side_effects=True, vmem_limit_bytes=62 * 1024 * 1024
        ),
        name="vcycle",
    )(*args.values())
    out = pl.pallas_call(
        finish,
        out_shape=(jax.ShapeDtypeStruct(field, jnp.float32),) * 2,
        in_specs=[hbm] * 2,
        out_specs=(hbm, hbm),
        scratch_shapes=[pltpu.VMEM(field, jnp.float32)] * 2 + [pltpu.SemaphoreType.DMA((2, 2, NV))],
        compiler_params=pltpu.CompilerParams(vmem_limit_bytes=62 * 1024 * 1024),
        name="finish",
    )(*out)
    return tuple(untile(x) for x in out)


def solution(mesh):
    in_specs = (
        P("tm", None, "space"),
        P("tm", None, "space"),
        P(None, None, None, "space"),
        P(None, None, "space"),
        P(None, "space"),
        P("space", None),
        P("space"),
    )
    out_specs = (P("tm", None, "space"), P("tm", None, "space"))
    step = functools.partial(body, mesh.shape["tm"], mesh.shape["space"])
    return jax.shard_map(step, mesh=mesh, in_specs=in_specs, out_specs=out_specs, check_vma=False)
```

```python
import functools

import jax
import jax.numpy as jnp
from jax import lax
from jax.experimental import pallas as pl
from jax.experimental.pallas import tpu as pltpu
from jax.sharding import PartitionSpec as P

NV = 5
BLK = 128
K = 6
BD = 16
H = 8
T = 8

WEIGHT = 0.5
COARSE = WEIGHT / 4.0
DAMP = 0.7
MESH = pl.DeviceIdType.MESH

FINE = ("f1", "f2", "f3", "f5", "f6")
SMALL = ("c0", "c1", "c2", "c3", "c4")
PARTS = ((0, 2), (2, 2), (4, 1))
RING = ("f1", "f2", "f3", "f5", "f6", "c1", "c2", "c3", "c4")


def roll(x, n):
    return pltpu.roll(x, n % T, axis=0)


def kernel(n_tm, n_space, names, *refs):
    r = dict(zip(names, refs))
    tm = lax.axis_index("tm")
    slab = lax.axis_index("space")
    core = lax.rem(slab, 2)
    near_dev = (tm, slab + 1 - 2 * core)
    far_slab = slab - 1 + 2 * core
    has_far = jnp.logical_and(far_slab >= 0, far_slab < n_space)
    far_dev = (tm, far_slab)
    next_dev = (lax.rem(tm + 1, n_tm), slab)
    prev_dev = (lax.rem(tm + n_tm - 1, n_tm), slab)
    near_slot = 1 - core
    far_slot = core
    nb, fl = r["nb"], r["fl"]
    jac, sb, dg = r["jac"], r["sb"], r["dg"]
    v, pre, rhs = r["v"], r["pre"], r["rhs"]
    cf, cc = r["cf"], r["cc"]
    corr, cpre, cd = r["corr"], r["cpre"], r["cd"]
    late, rank, others = r["late"], r["rank"], r["others"]
    base, aim, jf, jc = r["base"], r["aim"], r["jf"], r["jc"]

    sub = lax.broadcasted_iota(jnp.int32, (T, BLK), 0)
    sub4 = lax.rem(sub, 4)

    barrier = pltpu.get_barrier_semaphore()
    for dev in (near_dev, next_dev, prev_dev):
        pl.semaphore_signal(barrier, inc=1, device_id=dev, device_id_type=MESH)

    @pl.when(has_far)
    def _():
        pl.semaphore_signal(barrier, inc=1, device_id=far_dev, device_id_type=MESH)

    loads = {}
    for i, (src, dst) in enumerate(
        (
            ("fl_in", "fl"),
            ("v_in", "v"),
            ("nb_in", "nb"),
            ("jac_in", "jac"),
            ("rhs_in", "rhs"),
            ("sb_in", "sb"),
            ("dg_in", "dg"),
        )
    ):
        loads[dst] = pltpu.make_async_copy(r[src], r[dst], r["load_sem"].at[i])
        loads[dst].start()

    sem_index = {}
    for name in FINE + SMALL:
        for side in ("near", "far"):
            for part in PARTS if (name, side) == ("f3", "far") else (None,):
                sem_index[name, side, part] = len(sem_index)
    for name in RING:
        for side in ("ring0", "ring1"):
            sem_index[name, side, None] = len(sem_index)

    def copy_of(name, side, part=None):
        i = sem_index[name, side, part]
        if side in ("near", "far"):
            src, dst = r["face_out_" + name], r[side + "_in_" + name]
            dev = near_dev if side == "near" else far_dev
            if part:
                src, dst = src.at[pl.ds(*part)], dst.at[pl.ds(*part)]
        else:
            src, dst = (r["ring_%s_%s_%s" % (way, name, side[-1])] for way in ("out", "in"))
            dev = next_dev
        return pltpu.make_async_remote_copy(
            src_ref=src,
            dst_ref=dst,
            send_sem=r["send_sem"].at[i],
            recv_sem=r["recv_sem"].at[i],
            device_id=dev,
            device_id_type=MESH,
        )

    def send_far(name, part=None):
        @pl.when(has_far)
        def _():
            copy_of(name, "far", part).start()

    def send_faces(name):
        send_far(name)
        copy_of(name, "near").start()

    def wait(name, side):
        if side == "far":

            @pl.when(has_far)
            def _():
                for part in PARTS if name == "f3" else (None,):
                    copy_of(name, side, part).wait_recv()

        else:
            copy_of(name, side).wait_recv()

    def row(ref, idx, k):
        return ref[idx + (pl.ds(k, T, stride=0), slice(None))]

    def own_block(b, x, g, field, three_w, timed):
        acc = []
        for a in range(NV):
            t = g[a] - (row(dg, (b,), a) + three_w) * x[a]
            t = t + timed(x[a])
            for j in range(NV):
                if j != a:
                    t = t - row(sb, (a, b), j) * x[j]
            acc.append(t)
        for k in range(2, K):
            at = nb[k, b]
            p = [field[j, at] for j in range(NV)]
            for a in range(NV):
                for j in range(NV):
                    acc[a] = acc[a] - row(jac, (a, j, b), k) * p[j]
        return acc

    def timed_fine(x):
        zero = jnp.zeros_like(x)
        one = jnp.where(sub >= 1, roll(x, 1), zero)
        two = jnp.where(sub >= 2, roll(x, 2), zero)
        return (4.0 * WEIGHT) * one - WEIGHT * two

    def timed_coarse(x):
        return (4.0 * COARSE) * jnp.where(sub >= 4, roll(x, 4), jnp.zeros_like(x))

    def grouped(count, values_of, keep, width):
        def step(g, carry):
            at = [width * g + i for i in range(width)]
            got = [values_of(b) for b in at]
            for b, values in zip(at, got):
                keep(b, values)
            return carry

        lax.fori_loop(0, count // width, step, 0)

    def store(ref, b, values):
        for a in range(NV):
            ref[a, b] = values[a]

    def own(field, g, out, three_w, timed):
        def values_of(b):
            x = [field[j, b] for j in range(NV)]
            return own_block(b, x, [g[a, b] for a in range(NV)], field, three_w, timed)

        grouped(BD, values_of, functools.partial(store, out), 2)

    def rim(acc, b, field, slot):
        at = jnp.bitwise_and(nb[slot, b], H - 1)
        p = [field[j, at] for j in range(NV)]
        for a in range(NV):
            for j in range(NV):
                acc[a] = acc[a] - row(jac, (a, j, b), slot) * p[j]
        return acc

    def fold_rim(out, field, slot):
        def values_of(b):
            return rim([out[a, b] for a in range(NV)], b, field, slot)

        grouped(BD, values_of, functools.partial(store, out), 4)

    def place_fine(x, i):
        q = WEIGHT * (roll(x, 2) - jnp.where(sub == 0, 4.0 * roll(x, 1), jnp.zeros_like(x)))
        return roll(q, 2 * i) if i else q

    def place_coarse(x, i):
        return COARSE * jnp.where(sub >= 4, x, x - 4.0 * roll(x, 4))

    def ring_tile(four, place):
        tile = place(four[0], 0)
        for i in range(1, 4):
            mine = lax.div(sub, 2) == i if place is place_fine else sub4 == i
            tile = jnp.where(mine, place(four[i], i), tile)
        return tile

    def send_others(name, field, place):
        out = r["ring_out_" + name + "_1"]
        for g in range(2):
            got = [[field[a, others[4 * g + i]] for i in range(4)] for a in range(NV)]
            for a in range(NV):
                out[a, g] = ring_tile(got[a], place)
        copy_of(name, "ring1").start()

    def spread(turns, i):
        x = turns[-i]
        for u in range(1, 4):
            x = jnp.where(sub4 == u, turns[u - i], x)
        return x

    def turns_of(tile):
        return {d: (roll(tile, d) if d else tile) for d in range(-3, 4)}

    def open_ring(name, part, fine):
        wait(name, "ring%d" % part)
        src = r["ring_in_%s_%d" % (name, part)]

        def body(a, carry):
            got = []
            for g in range(2):
                tile = src[a, g]
                turns = None if fine else turns_of(tile)
                for i in range(4):
                    if fine:
                        q = roll(tile, T - 2 * i) if i else tile
                        got.append(jnp.where(sub < 2, q, jnp.zeros_like(q)))
                    else:
                        got.append(spread(turns, i))
            for i in range(H):
                late[a, H * part + i] = got[i]
            return carry

        lax.fori_loop(0, NV, body, 0)

    def unpack(name, side):
        wait(name, side)
        src, out = r[side + "_in_" + name], r["rim_" + side]

        def body(a, carry):
            got = []
            for g in range(H // 4):
                turns = turns_of(src[a, g])
                got += [spread(turns, i) for i in range(4)]
            for i in range(H):
                out[a, i] = got[i]
            return carry

        lax.fori_loop(0, NV, body, 0)
        return out

    def mean4(x):
        x = x + jnp.where(lax.rem(sub, 2) == 0, roll(x, -1), roll(x, 1))
        x = x + jnp.where(sub4 < 2, roll(x, -2), roll(x, 2))
        return 0.25 * x

    def faces(value_of, place, ring_name, full=None, small=None, average=False):
        kept = r["face_out_" + full] if full else r["face_kept"]
        for g in range(2):
            got = [value_of(4 * g + i) for i in range(4)]
            for a in range(NV):
                for i in range(4):
                    kept[a, 4 * g + i] = got[i][a]
                if small:
                    four = [mean4(x[a]) if average else x[a] for x in got]
                    tile = four[0]
                    for i in range(1, 4):
                        tile = jnp.where(sub4 == i, four[i], tile)
                    r["face_out_" + small][a, g] = tile
        send_faces(small or full)
        for g in range(2):
            for a in range(NV):
                four = [kept[a, 4 * g + i] for i in range(4)]
                r["ring_out_" + ring_name + "_0"][a, g] = ring_tile(four, place)
        copy_of(ring_name, "ring0").start()

    def prepare(values_of):
        def step(g, carry):
            at = [2 * g, 2 * g + 1]
            got = [values_of(h, fl[h]) for h in at]
            for h, values in zip(at, got):
                store(base, h, values)
            return carry

        lax.fori_loop(0, H // 2, step, 0)

    def prepare_sweep(field, p, scale):
        def values_of(h, b):
            return [field[a, b] + scale[a, b] * (p[a, b] - late[a, h]) for a in range(NV)]

        prepare(values_of)

    def face_value(table, far, h):
        at = aim[h]
        p = [far[j, at] for j in range(NV)]
        values = []
        for a in range(NV):
            q = [table[h, NV * a + j] * p[j] for j in range(NV)]
            values.append(base[a, h] - ((q[0] + q[1]) + (q[2] + q[3]) + q[4]))
        return values

    def swept(field, p, scale, far, b):
        at = rank[b]
        acc = rim([p[a, b] - late[a, at] for a in range(NV)], b, far, far_slot)
        return [field[a, b] + scale[a, b] * acc[a] for a in range(NV)]

    def sweep(field, p, scale, far):
        grouped(BD, functools.partial(swept, field, p, scale, far), functools.partial(store, field), 4)

    @pl.when(jnp.logical_not(has_far))
    def _():
        for name in FINE + SMALL:
            ref = r["far_in_" + name]

            def clear(a, carry, ref=ref):
                for i in range(ref.shape[1]):
                    ref[a, i] = jnp.zeros((T, BLK), jnp.float32)
                return carry

            lax.fori_loop(0, NV, clear, 0)

    loads["fl"].wait()
    loads["v"].wait()
    pl.semaphore_wait(barrier, jnp.where(has_far, 4, 3))
    faces(lambda h: [v[a, fl[h]] for a in range(NV)], place_fine, "f1", full="f1")

    def rank_of(b, count):
        at = jnp.minimum(H + count, BD - 1)
        for h in range(H):
            at = jnp.where(fl[h] == b, h, at)
        rank[b] = at
        return jnp.where(at >= H, count + 1, count)

    lax.fori_loop(0, BD, rank_of, jnp.int32(0))

    def other_of(i, carry):
        b = jnp.int32(0)
        for c in range(BD):
            b = jnp.where(rank[c] == H + i, c, b)
        others[i] = b
        return carry

    lax.fori_loop(0, H, other_of, 0)
    send_others("f1", v, place_fine)
    for name in ("nb", "jac", "rhs", "sb", "dg"):
        loads[name].wait()

    def scales(b):
        d = [row(dg, (b,), a) for a in range(NV)]
        return [DAMP / (3.0 * WEIGHT + x) for x in d] + [DAMP / (3.0 * COARSE + x) for x in d]

    def keep_scales(b, values):
        store(cf, b, values[:NV])
        store(cc, b, values[NV:])

    grouped(BD, scales, keep_scales, 2)

    def scaled(h, carry):
        b = fl[h]
        aim[h] = jnp.bitwise_and(nb[far_slot, b], H - 1)
        for a in range(NV):
            fine, coarse = cf[a, b], cc[a, b]
            x = [row(jac, (a, j, b), far_slot) for j in range(NV)]
            for j in range(NV):
                jf[h, NV * a + j] = fine * x[j]
                jc[h, NV * a + j] = coarse * x[j]
        return carry

    lax.fori_loop(0, H, scaled, 0)

    def arrive(name, out):
        wait(name, "near")
        fold_rim(out, r["near_in_" + name], near_slot)
        open_ring(name, 0, True)
        prepare_sweep(v, out, cf)
        wait(name, "far")
        return r["far_in_" + name]

    own(v, rhs, pre, 3.0 * WEIGHT, timed_fine)
    far = arrive("f1", pre)
    faces(functools.partial(face_value, jf, far), place_fine, "f2", full="f2")
    open_ring("f1", 1, True)
    sweep(v, pre, cf, far)
    send_others("f2", v, place_fine)
    own(v, rhs, pre, 3.0 * WEIGHT, timed_fine)
    far = arrive("f2", pre)
    faces(functools.partial(face_value, jf, far), place_fine, "f3", full="f3", small="c0", average=True)
    open_ring("f2", 1, True)
    sweep(v, pre, cf, far)
    send_others("f3", v, place_fine)
    send_far("f3", PARTS[0])
    copy_of("f3", "near").start()

    own(v, rhs, pre, 3.0 * WEIGHT, timed_fine)
    grouped(BD, lambda b: [mean4(pre[a, b]) for a in range(NV)], functools.partial(store, cpre), 2)
    fold_rim(cpre, unpack("c0", "near"), near_slot)
    open_ring("f3", 0, True)
    prepare(lambda h, b: [cc[a, b] * (cpre[a, b] - mean4(late[a, h])) for a in range(NV)])
    far = unpack("c0", "far")

    def first(b):
        q = [late[a, rank[b]] for a in range(NV)]
        acc = rim([cpre[a, b] - mean4(q[a]) for a in range(NV)], b, far, far_slot)
        return acc + [cc[a, b] * acc[a] for a in range(NV)] + [pre[a, b] - q[a] for a in range(NV)]

    def keep_first(b, values):
        store(cd, b, values[:NV])
        store(corr, b, values[NV : 2 * NV])
        store(pre, b, values[2 * NV :])

    faces(functools.partial(face_value, jc, far), place_coarse, "c1", small="c1")
    open_ring("f3", 1, True)
    grouped(BD, first, keep_first, 2)
    send_others("c1", corr, place_coarse)
    send_far("f3", PARTS[1])

    for name, later in (("c1", "c2"), ("c2", "c3"), ("c3", "c4")):
        place = place_fine if later == "c4" else place_coarse
        own(corr, cd, cpre, 3.0 * COARSE, timed_coarse)
        fold_rim(cpre, unpack(name, "near"), near_slot)
        open_ring(name, 0, False)
        if name == "c3":
            for side, slot in (("near", near_slot), ("far", far_slot)):
                wait("f3", side)
                fold_rim(pre, r[side + "_in_f3"], slot)
        prepare_sweep(corr, cpre, cc)
        far = unpack(name, "far")
        faces(functools.partial(face_value, jc, far), place, later, small=later)
        open_ring(name, 1, False)
        sweep(corr, cpre, cc, far)
        send_others(later, corr, place)
        if later == "c2":
            send_far("f3", PARTS[2])

    own(corr, pre, pre, 3.0 * WEIGHT, timed_fine)
    grouped(BD, lambda b: [v[a, b] + corr[a, b] for a in range(NV)], functools.partial(store, v), 4)
    fold_rim(pre, unpack("c4", "near"), near_slot)
    open_ring("c4", 0, True)
    prepare_sweep(v, pre, cf)
    far = unpack("c4", "far")
    for name, later in (("c4", "f5"), ("f5", "f6")):
        faces(functools.partial(face_value, jf, far), place_fine, later, full=later)
        open_ring(name, 1, True)
        sweep(v, pre, cf, far)
        send_others(later, v, place_fine)
        if later == "f6":
            save_v = pltpu.make_async_copy(v, r["v_out"], r["load_sem"].at[7])
            save_v.start()
        own(v, rhs, pre, 3.0 * WEIGHT, timed_fine)
        if later == "f5":
            far = arrive(later, pre)
    wait("f6", "near")
    fold_rim(pre, r["near_in_f6"], near_slot)
    open_ring("f6", 0, True)
    open_ring("f6", 1, True)
    grouped(
        BD,
        lambda b: [pre[a, b] - late[a, rank[b]] for a in range(NV)],
        functools.partial(store, pre),
        4,
    )
    wait("f6", "far")
    save_r = []
    for g in range(4):
        at = [4 * g + i for i in range(4)]
        got = [rim([pre[a, b] for a in range(NV)], b, r["far_in_f6"], far_slot) for b in at]
        for b, values in zip(at, got):
            store(pre, b, values)
        quarter = (slice(None), pl.ds(4 * g, 4))
        save_r.append(
            pltpu.make_async_copy(pre.at[quarter], r["r_out"].at[quarter], r["load_sem"].at[8 + g])
        )
        save_r[-1].start()
    for key in sem_index:
        if key[1] == "far":

            @pl.when(has_far)
            def _(key=key):
                copy_of(*key).wait_send()

        else:
            copy_of(*key).wait_send()
    save_v.wait()
    for save in save_r:
        save.wait()


def finish(*refs):
    ins, outs, sems = refs[:2], refs[2:4], refs[4]
    parts = [
        pltpu.make_async_copy(ins[i].at[a], outs[i].at[a], sems.at[i, a])
        for i in range(2)
        for a in range(NV)
    ]
    for part in parts:
        part.start()
    for part in parts:
        part.wait()


def body(n_tm, n_space, iterate, right_side, jacobian, self_block, cell_diag, neighbours, face_list):
    def tiles(x):
        return x.reshape(T, NV, BD, BLK).transpose(1, 2, 0, 3)

    def untile(x):
        return x.transpose(2, 0, 1, 3).reshape(T, NV, BD * BLK)

    args = {
        "nb_in": neighbours.T,
        "fl_in": face_list,
        "v_in": tiles(iterate),
        "jac_in": jacobian.reshape(K, NV, NV, BD, BLK).transpose(1, 2, 3, 0, 4),
        "rhs_in": tiles(right_side),
        "sb_in": self_block.reshape(NV, NV, BD, BLK).transpose(0, 2, 1, 3),
        "dg_in": cell_diag.reshape(NV, BD, BLK).transpose(1, 0, 2),
    }
    field = (NV, BD, T, BLK)
    face = (NV, H, T, BLK)
    small = (NV, H // 4, T, BLK)
    scratch = {
        "v": field,
        "jac": (NV, NV, BD, K, BLK),
        "rhs": field,
        "sb": (NV, BD, NV, BLK),
        "dg": (BD, NV, BLK),
        "pre": field,
        "cf": field,
        "cc": field,
        "corr": field,
        "cpre": field,
        "cd": field,
        "late": field,
        "face_kept": face,
        "base": face,
        "jf": (H, NV * NV, T, BLK),
        "jc": (H, NV * NV, T, BLK),
        "rim_near": face,
        "rim_far": face,
    }
    for name in FINE + SMALL:
        for key in ("face_out_", "near_in_", "far_in_"):
            scratch[key + name] = face if name in FINE else small
    for name in RING:
        for key in ("ring_out_", "ring_in_"):
            for part in ("_0", "_1"):
                scratch[key + name + part] = small
    n_sems = 2 * len(FINE + SMALL) + len(PARTS) - 1 + 2 * len(RING)
    names = list(args) + ["v_out", "r_out"] + list(scratch) + ["fl", "nb", "aim", "rank", "others", "load_sem", "send_sem", "recv_sem"]
    hbm = pl.BlockSpec(memory_space=pltpu.HBM)
    out = pl.pallas_call(
        functools.partial(kernel, n_tm, n_space, names),
        out_shape=(jax.ShapeDtypeStruct(field, jnp.float32),) * 2,
        in_specs=[hbm] * 7,
        out_specs=(hbm, hbm),
        scratch_shapes=[pltpu.VMEM(shape, jnp.float32) for shape in scratch.values()]
        + [
            pltpu.SMEM((H,), jnp.int32),
            pltpu.SMEM((K, BD), jnp.int32),
            pltpu.SMEM((H,), jnp.int32),
            pltpu.SMEM((BD,), jnp.int32),
            pltpu.SMEM((H,), jnp.int32),
            pltpu.SemaphoreType.DMA((12,)),
            pltpu.SemaphoreType.DMA((n_sems,)),
            pltpu.SemaphoreType.DMA((n_sems,)),
        ],
        compiler_params=pltpu.CompilerParams(
            collective_id=0, has_side_effects=True, vmem_limit_bytes=44 * 1024 * 1024
        ),
        name="vcycle",
    )(*[pltpu.with_memory_space_constraint(x, pltpu.HBM) for x in args.values()])
    out = pl.pallas_call(
        finish,
        out_shape=(pltpu.HBM(field, jnp.float32),) * 2,
        in_specs=[pl.BlockSpec(memory_space=pl.ANY)] * 2,
        out_specs=(hbm, hbm),
        scratch_shapes=[pltpu.SemaphoreType.DMA((2, NV))],
        compiler_params=pltpu.CompilerParams(vmem_limit_bytes=44 * 1024 * 1024),
        name="finish",
    )(*out)
    return tuple(untile(x) for x in out)


def solution(mesh):
    in_specs = (
        P("tm", None, "space"),
        P("tm", None, "space"),
        P(None, None, None, "space"),
        P(None, None, "space"),
        P(None, "space"),
        P("space", None),
        P("space"),
    )
    out_specs = (P("tm", None, "space"), P("tm", None, "space"))
    step = functools.partial(body, mesh.shape["tm"], mesh.shape["space"])
    return jax.shard_map(step, mesh=mesh, in_specs=in_specs, out_specs=out_specs, check_vma=False)
```

```python
import functools

import jax
import jax.numpy as jnp
from jax import lax
from jax.experimental import pallas as pl
from jax.experimental.pallas import tpu as pltpu
from jax.sharding import PartitionSpec as P

NV = 5
BLK = 128
K = 6
BD = 16
H = 8
T = 8

WEIGHT = 0.5
COARSE = WEIGHT / 4.0
DAMP = 0.7
MESH = pl.DeviceIdType.MESH

FINE = ("f1", "f2", "f3", "f5", "f6")
SMALL = ("c0", "c1", "c2", "c3", "c4")
PARTS = ((0, 2), (2, 2), (4, 1))
RING = ("f1", "f2", "f3", "f5", "f6", "c1", "c2", "c3", "c4")


def roll(x, n):
    return pltpu.roll(x, n % T, axis=0)


def kernel(n_tm, n_space, names, *refs):
    r = dict(zip(names, refs))
    tm = lax.axis_index("tm")
    slab = lax.axis_index("space")
    core = lax.rem(slab, 2)
    near_dev = (tm, slab + 1 - 2 * core)
    far_slab = slab - 1 + 2 * core
    has_far = jnp.logical_and(far_slab >= 0, far_slab < n_space)
    far_dev = (tm, far_slab)
    next_dev = (lax.rem(tm + 1, n_tm), slab)
    prev_dev = (lax.rem(tm + n_tm - 1, n_tm), slab)
    near_slot = 1 - core
    far_slot = core
    nb, fl = r["nb"], r["fl"]
    jac, sb, dg = r["jac"], r["sb"], r["dg"]
    v, pre, rhs = r["v"], r["pre"], r["rhs"]
    cf, cc = r["cf"], r["cc"]
    corr, cpre, cd = r["corr"], r["cpre"], r["cd"]
    late, rank, others = r["late"], r["rank"], r["others"]
    base, aim, jf, jc = r["base"], r["aim"], r["jf"], r["jc"]

    sub = lax.broadcasted_iota(jnp.int32, (T, BLK), 0)
    sub4 = lax.rem(sub, 4)

    barrier = pltpu.get_barrier_semaphore()
    for dev in (near_dev, next_dev, prev_dev):
        pl.semaphore_signal(barrier, inc=1, device_id=dev, device_id_type=MESH)

    @pl.when(has_far)
    def _():
        pl.semaphore_signal(barrier, inc=1, device_id=far_dev, device_id_type=MESH)

    loads = {}
    for i, (src, dst) in enumerate(
        (
            ("fl_in", "fl"),
            ("v_in", "v"),
            ("nb_in", "nb"),
            ("jac_in", "jac"),
            ("rhs_in", "rhs"),
            ("sb_in", "sb"),
            ("dg_in", "dg"),
        )
    ):
        loads[dst] = pltpu.make_async_copy(r[src], r[dst], r["load_sem"].at[i])
        loads[dst].start()

    sem_index = {}
    for name in FINE + SMALL:
        for side in ("near", "far"):
            for part in PARTS if (name, side) == ("f3", "far") else (None,):
                sem_index[name, side, part] = len(sem_index)
    for name in RING:
        for side in ("ring0", "ring1"):
            sem_index[name, side, None] = len(sem_index)

    def copy_of(name, side, part=None):
        i = sem_index[name, side, part]
        if side in ("near", "far"):
            src, dst = r["face_out_" + name], r[side + "_in_" + name]
            dev = near_dev if side == "near" else far_dev
            if part:
                src, dst = src.at[pl.ds(*part)], dst.at[pl.ds(*part)]
        else:
            src, dst = (r["ring_%s_%s_%s" % (way, name, side[-1])] for way in ("out", "in"))
            dev = next_dev
        return pltpu.make_async_remote_copy(
            src_ref=src,
            dst_ref=dst,
            send_sem=r["send_sem"].at[i],
            recv_sem=r["recv_sem"].at[i],
            device_id=dev,
            device_id_type=MESH,
        )

    def send_far(name, part=None):
        @pl.when(has_far)
        def _():
            copy_of(name, "far", part).start()

    def send_faces(name):
        send_far(name)
        copy_of(name, "near").start()

    def wait(name, side):
        if side == "far":

            @pl.when(has_far)
            def _():
                for part in PARTS if name == "f3" else (None,):
                    copy_of(name, side, part).wait_recv()

        else:
            copy_of(name, side).wait_recv()

    def row(ref, idx, k):
        return ref[idx + (pl.ds(k, T, stride=0), slice(None))]

    def own_block(b, x, g, field, three_w, timed):
        acc = []
        for a in range(NV):
            t = g[a] - (row(dg, (b,), a) + three_w) * x[a]
            t = t + timed(x[a])
            for j in range(NV):
                if j != a:
                    t = t - row(sb, (a, b), j) * x[j]
            acc.append(t)
        for k in range(2, K):
            at = nb[k, b]
            p = [field[j, at] for j in range(NV)]
            for a in range(NV):
                for j in range(NV):
                    acc[a] = acc[a] - row(jac, (a, j, b), k) * p[j]
        return acc

    def timed_fine(x):
        zero = jnp.zeros_like(x)
        one = jnp.where(sub >= 1, roll(x, 1), zero)
        two = jnp.where(sub >= 2, roll(x, 2), zero)
        return (4.0 * WEIGHT) * one - WEIGHT * two

    def timed_coarse(x):
        return (4.0 * COARSE) * jnp.where(sub >= 4, roll(x, 4), jnp.zeros_like(x))

    def grouped(count, values_of, keep, width):
        def step(g, carry):
            at = [width * g + i for i in range(width)]
            got = [values_of(b) for b in at]
            for b, values in zip(at, got):
                keep(b, values)
            return carry

        lax.fori_loop(0, count // width, step, 0)

    def store(ref, b, values):
        for a in range(NV):
            ref[a, b] = values[a]

    def own(field, g, out, three_w, timed):
        def values_of(b):
            x = [field[j, b] for j in range(NV)]
            return own_block(b, x, [g[a, b] for a in range(NV)], field, three_w, timed)

        grouped(BD, values_of, functools.partial(store, out), 2)

    def rim(acc, b, field, slot):
        at = jnp.bitwise_and(nb[slot, b], H - 1)
        p = [field[j, at] for j in range(NV)]
        for a in range(NV):
            for j in range(NV):
                acc[a] = acc[a] - row(jac, (a, j, b), slot) * p[j]
        return acc

    def fold_rim(out, field, slot):
        def values_of(b):
            return rim([out[a, b] for a in range(NV)], b, field, slot)

        grouped(BD, values_of, functools.partial(store, out), 4)

    def place_fine(x, i):
        q = WEIGHT * (roll(x, 2) - jnp.where(sub == 0, 4.0 * roll(x, 1), jnp.zeros_like(x)))
        return roll(q, 2 * i) if i else q

    def place_coarse(x, i):
        return COARSE * jnp.where(sub >= 4, x, x - 4.0 * roll(x, 4))

    def ring_tile(four, place):
        tile = place(four[0], 0)
        for i in range(1, 4):
            mine = lax.div(sub, 2) == i if place is place_fine else sub4 == i
            tile = jnp.where(mine, place(four[i], i), tile)
        return tile

    def send_others(name, field, place):
        out = r["ring_out_" + name + "_1"]
        for g in range(2):
            got = [[field[a, others[4 * g + i]] for i in range(4)] for a in range(NV)]
            for a in range(NV):
                out[a, g] = ring_tile(got[a], place)
        copy_of(name, "ring1").start()

    def spread(turns, i):
        x = turns[-i]
        for u in range(1, 4):
            x = jnp.where(sub4 == u, turns[u - i], x)
        return x

    def turns_of(tile):
        return {d: (roll(tile, d) if d else tile) for d in range(-3, 4)}

    def open_ring(name, part, fine):
        wait(name, "ring%d" % part)
        src = r["ring_in_%s_%d" % (name, part)]

        def body(a, carry):
            got = []
            for g in range(2):
                tile = src[a, g]
                turns = None if fine else turns_of(tile)
                for i in range(4):
                    if fine:
                        q = roll(tile, T - 2 * i) if i else tile
                        got.append(jnp.where(sub < 2, q, jnp.zeros_like(q)))
                    else:
                        got.append(spread(turns, i))
            for i in range(H):
                late[a, H * part + i] = got[i]
            return carry

        lax.fori_loop(0, NV, body, 0)

    def unpack(name, side):
        wait(name, side)
        src, out = r[side + "_in_" + name], r["rim_" + side]

        def body(a, carry):
            got = []
            for g in range(H // 4):
                turns = turns_of(src[a, g])
                got += [spread(turns, i) for i in range(4)]
            for i in range(H):
                out[a, i] = got[i]
            return carry

        lax.fori_loop(0, NV, body, 0)
        return out

    def mean4(x):
        x = x + jnp.where(lax.rem(sub, 2) == 0, roll(x, -1), roll(x, 1))
        x = x + jnp.where(sub4 < 2, roll(x, -2), roll(x, 2))
        return 0.25 * x

    def faces(value_of, place, ring_name, full=None, small=None, average=False):
        kept = r["face_out_" + full] if full else r["face_kept"]
        for g in range(2):
            got = [value_of(4 * g + i) for i in range(4)]
            for a in range(NV):
                for i in range(4):
                    kept[a, 4 * g + i] = got[i][a]
                if small:
                    four = [mean4(x[a]) if average else x[a] for x in got]
                    tile = four[0]
                    for i in range(1, 4):
                        tile = jnp.where(sub4 == i, four[i], tile)
                    r["face_out_" + small][a, g] = tile
        if not small:
            send_faces(full)
        for g in range(2):
            for a in range(NV):
                four = [kept[a, 4 * g + i] for i in range(4)]
                r["ring_out_" + ring_name + "_0"][a, g] = ring_tile(four, place)
        copy_of(ring_name, "ring0").start()
        if small:
            send_faces(small)

    def prepare(values_of):
        def step(g, carry):
            at = [2 * g, 2 * g + 1]
            got = [values_of(h, fl[h]) for h in at]
            for h, values in zip(at, got):
                store(base, h, values)
            return carry

        lax.fori_loop(0, H // 2, step, 0)

    def prepare_sweep(field, p, scale):
        def values_of(h, b):
            return [field[a, b] + scale[a, b] * (p[a, b] - late[a, h]) for a in range(NV)]

        prepare(values_of)

    def face_value(table, far, h):
        at = aim[h]
        p = [far[j, at] for j in range(NV)]
        values = []
        for a in range(NV):
            q = [table[h, NV * a + j] * p[j] for j in range(NV)]
            values.append(base[a, h] - ((q[0] + q[1]) + (q[2] + q[3]) + q[4]))
        return values

    def swept(field, p, scale, far, b):
        at = rank[b]
        acc = rim([p[a, b] - late[a, at] for a in range(NV)], b, far, far_slot)
        return [field[a, b] + scale[a, b] * acc[a] for a in range(NV)]

    def sweep(field, p, scale, far):
        grouped(BD, functools.partial(swept, field, p, scale, far), functools.partial(store, field), 4)

    @pl.when(jnp.logical_not(has_far))
    def _():
        for name in FINE + SMALL:
            ref = r["far_in_" + name]

            def clear(a, carry, ref=ref):
                for i in range(ref.shape[1]):
                    ref[a, i] = jnp.zeros((T, BLK), jnp.float32)
                return carry

            lax.fori_loop(0, NV, clear, 0)

    loads["fl"].wait()
    loads["v"].wait()
    pl.semaphore_wait(barrier, jnp.where(has_far, 4, 3))
    faces(lambda h: [v[a, fl[h]] for a in range(NV)], place_fine, "f1", full="f1")

    def rank_of(b, count):
        at = jnp.minimum(H + count, BD - 1)
        for h in range(H):
            at = jnp.where(fl[h] == b, h, at)
        rank[b] = at
        return jnp.where(at >= H, count + 1, count)

    lax.fori_loop(0, BD, rank_of, jnp.int32(0))

    def other_of(i, carry):
        b = jnp.int32(0)
        for c in range(BD):
            b = jnp.where(rank[c] == H + i, c, b)
        others[i] = b
        return carry

    lax.fori_loop(0, H, other_of, 0)
    send_others("f1", v, place_fine)
    for name in ("nb", "jac", "rhs", "sb", "dg"):
        loads[name].wait()

    def scales(b):
        d = [row(dg, (b,), a) for a in range(NV)]
        return [DAMP / (3.0 * WEIGHT + x) for x in d] + [DAMP / (3.0 * COARSE + x) for x in d]

    def keep_scales(b, values):
        store(cf, b, values[:NV])
        store(cc, b, values[NV:])

    grouped(BD, scales, keep_scales, 2)

    def scaled(h, carry):
        b = fl[h]
        aim[h] = jnp.bitwise_and(nb[far_slot, b], H - 1)
        for a in range(NV):
            fine, coarse = cf[a, b], cc[a, b]
            x = [row(jac, (a, j, b), far_slot) for j in range(NV)]
            for j in range(NV):
                jf[h, NV * a + j] = fine * x[j]
                jc[h, NV * a + j] = coarse * x[j]
        return carry

    lax.fori_loop(0, H, scaled, 0)

    def arrive(name, out):
        wait(name, "near")
        fold_rim(out, r["near_in_" + name], near_slot)
        open_ring(name, 0, True)
        prepare_sweep(v, out, cf)
        wait(name, "far")
        return r["far_in_" + name]

    own(v, rhs, pre, 3.0 * WEIGHT, timed_fine)
    far = arrive("f1", pre)
    faces(functools.partial(face_value, jf, far), place_fine, "f2", full="f2")
    open_ring("f1", 1, True)
    sweep(v, pre, cf, far)
    send_others("f2", v, place_fine)
    own(v, rhs, pre, 3.0 * WEIGHT, timed_fine)
    far = arrive("f2", pre)
    faces(functools.partial(face_value, jf, far), place_fine, "f3", full="f3", small="c0", average=True)
    open_ring("f2", 1, True)
    sweep(v, pre, cf, far)
    send_others("f3", v, place_fine)
    send_far("f3", PARTS[0])
    copy_of("f3", "near").start()

    own(v, rhs, pre, 3.0 * WEIGHT, timed_fine)
    grouped(BD, lambda b: [mean4(pre[a, b]) for a in range(NV)], functools.partial(store, cpre), 2)
    fold_rim(cpre, unpack("c0", "near"), near_slot)
    open_ring("f3", 0, True)
    prepare(lambda h, b: [cc[a, b] * (cpre[a, b] - mean4(late[a, h])) for a in range(NV)])
    far = unpack("c0", "far")

    def first(b):
        q = [late[a, rank[b]] for a in range(NV)]
        acc = rim([cpre[a, b] - mean4(q[a]) for a in range(NV)], b, far, far_slot)
        return acc + [cc[a, b] * acc[a] for a in range(NV)] + [pre[a, b] - q[a] for a in range(NV)]

    def keep_first(b, values):
        store(cd, b, values[:NV])
        store(corr, b, values[NV : 2 * NV])
        store(pre, b, values[2 * NV :])

    faces(functools.partial(face_value, jc, far), place_coarse, "c1", small="c1")
    open_ring("f3", 1, True)
    grouped(BD, first, keep_first, 2)
    send_others("c1", corr, place_coarse)
    send_far("f3", PARTS[1])

    for name, later in (("c1", "c2"), ("c2", "c3"), ("c3", "c4")):
        place = place_fine if later == "c4" else place_coarse
        own(corr, cd, cpre, 3.0 * COARSE, timed_coarse)
        fold_rim(cpre, unpack(name, "near"), near_slot)
        open_ring(name, 0, False)
        if name == "c3":
            for side, slot in (("near", near_slot), ("far", far_slot)):
                wait("f3", side)
                fold_rim(pre, r[side + "_in_f3"], slot)
        prepare_sweep(corr, cpre, cc)
        far = unpack(name, "far")
        faces(functools.partial(face_value, jc, far), place, later, small=later)
        open_ring(name, 1, False)
        sweep(corr, cpre, cc, far)
        send_others(later, corr, place)
        if later == "c2":
            send_far("f3", PARTS[2])

    own(corr, pre, pre, 3.0 * WEIGHT, timed_fine)
    grouped(BD, lambda b: [v[a, b] + corr[a, b] for a in range(NV)], functools.partial(store, v), 4)
    fold_rim(pre, unpack("c4", "near"), near_slot)
    open_ring("c4", 0, True)
    prepare_sweep(v, pre, cf)
    far = unpack("c4", "far")
    for name, later in (("c4", "f5"), ("f5", "f6")):
        faces(functools.partial(face_value, jf, far), place_fine, later, full=later)
        open_ring(name, 1, True)
        sweep(v, pre, cf, far)
        send_others(later, v, place_fine)
        if later == "f6":
            save_v = pltpu.make_async_copy(v, r["v_out"], r["load_sem"].at[7])
            save_v.start()
        own(v, rhs, pre, 3.0 * WEIGHT, timed_fine)
        if later == "f5":
            far = arrive(later, pre)
    wait("f6", "near")
    fold_rim(pre, r["near_in_f6"], near_slot)
    open_ring("f6", 0, True)
    open_ring("f6", 1, True)
    grouped(
        BD,
        lambda b: [pre[a, b] - late[a, rank[b]] for a in range(NV)],
        functools.partial(store, pre),
        4,
    )
    wait("f6", "far")
    save_r = []
    for g in range(4):
        at = [4 * g + i for i in range(4)]
        got = [rim([pre[a, b] for a in range(NV)], b, r["far_in_f6"], far_slot) for b in at]
        for b, values in zip(at, got):
            store(pre, b, values)
        quarter = (slice(None), pl.ds(4 * g, 4))
        save_r.append(
            pltpu.make_async_copy(pre.at[quarter], r["r_out"].at[quarter], r["load_sem"].at[8 + g])
        )
        save_r[-1].start()
    for key in sem_index:
        if key[1] == "far":

            @pl.when(has_far)
            def _(key=key):
                copy_of(*key).wait_send()

        else:
            copy_of(*key).wait_send()
    save_v.wait()
    for save in save_r:
        save.wait()


def finish(*refs):
    ins, outs, sems = refs[:2], refs[2:4], refs[4]
    parts = [
        pltpu.make_async_copy(ins[i].at[a], outs[i].at[a], sems.at[i, a])
        for i in range(2)
        for a in range(NV)
    ]
    for part in parts:
        part.start()
    for part in parts:
        part.wait()


def body(n_tm, n_space, iterate, right_side, jacobian, self_block, cell_diag, neighbours, face_list):
    def tiles(x):
        return x.reshape(T, NV, BD, BLK).transpose(1, 2, 0, 3)

    def untile(x):
        return x.transpose(2, 0, 1, 3).reshape(T, NV, BD * BLK)

    args = {
        "nb_in": neighbours.T,
        "fl_in": face_list,
        "v_in": tiles(iterate),
        "jac_in": jacobian.reshape(K, NV, NV, BD, BLK).transpose(1, 2, 3, 0, 4),
        "rhs_in": tiles(right_side),
        "sb_in": self_block.reshape(NV, NV, BD, BLK).transpose(0, 2, 1, 3),
        "dg_in": cell_diag.reshape(NV, BD, BLK).transpose(1, 0, 2),
    }
    field = (NV, BD, T, BLK)
    face = (NV, H, T, BLK)
    small = (NV, H // 4, T, BLK)
    scratch = {
        "v": field,
        "jac": (NV, NV, BD, K, BLK),
        "rhs": field,
        "sb": (NV, BD, NV, BLK),
        "dg": (BD, NV, BLK),
        "pre": field,
        "cf": field,
        "cc": field,
        "corr": field,
        "cpre": field,
        "cd": field,
        "late": field,
        "face_kept": face,
        "base": face,
        "jf": (H, NV * NV, T, BLK),
        "jc": (H, NV * NV, T, BLK),
        "rim_near": face,
        "rim_far": face,
    }
    for name in FINE + SMALL:
        for key in ("face_out_", "near_in_", "far_in_"):
            scratch[key + name] = face if name in FINE else small
    for name in RING:
        for key in ("ring_out_", "ring_in_"):
            for part in ("_0", "_1"):
                scratch[key + name + part] = small
    n_sems = 2 * len(FINE + SMALL) + len(PARTS) - 1 + 2 * len(RING)
    names = list(args) + ["v_out", "r_out"] + list(scratch) + ["fl", "nb", "aim", "rank", "others", "load_sem", "send_sem", "recv_sem"]
    hbm = pl.BlockSpec(memory_space=pltpu.HBM)
    out = pl.pallas_call(
        functools.partial(kernel, n_tm, n_space, names),
        out_shape=(jax.ShapeDtypeStruct(field, jnp.float32),) * 2,
        in_specs=[hbm] * 7,
        out_specs=(hbm, hbm),
        scratch_shapes=[pltpu.VMEM(shape, jnp.float32) for shape in scratch.values()]
        + [
            pltpu.SMEM((H,), jnp.int32),
            pltpu.SMEM((K, BD), jnp.int32),
            pltpu.SMEM((H,), jnp.int32),
            pltpu.SMEM((BD,), jnp.int32),
            pltpu.SMEM((H,), jnp.int32),
            pltpu.SemaphoreType.DMA((12,)),
            pltpu.SemaphoreType.DMA((n_sems,)),
            pltpu.SemaphoreType.DMA((n_sems,)),
        ],
        compiler_params=pltpu.CompilerParams(
            collective_id=0, has_side_effects=True, vmem_limit_bytes=44 * 1024 * 1024
        ),
        name="vcycle",
    )(*[pltpu.with_memory_space_constraint(x, pltpu.HBM) for x in args.values()])
    out = pl.pallas_call(
        finish,
        out_shape=(pltpu.HBM(field, jnp.float32),) * 2,
        in_specs=[pl.BlockSpec(memory_space=pl.ANY)] * 2,
        out_specs=(hbm, hbm),
        scratch_shapes=[pltpu.SemaphoreType.DMA((2, NV))],
        compiler_params=pltpu.CompilerParams(vmem_limit_bytes=44 * 1024 * 1024),
        name="finish",
    )(*out)
    return tuple(untile(x) for x in out)


def solution(mesh):
    in_specs = (
        P("tm", None, "space"),
        P("tm", None, "space"),
        P(None, None, None, "space"),
        P(None, None, "space"),
        P(None, "space"),
        P("space", None),
        P("space"),
    )
    out_specs = (P("tm", None, "space"), P("tm", None, "space"))
    step = functools.partial(body, mesh.shape["tm"], mesh.shape["space"])
    return jax.shard_map(step, mesh=mesh, in_specs=in_specs, out_specs=out_specs, check_vma=False)
```
